256 devices in a mesh: tile: 128 (over x, z, y), frame: 2 (over core).
Axes of the slice: x: 4, y: 4, z: 8, core: 2. Of those that a mesh axis runs over, the one named last changes fastest.
Arguments:
- movie_block: bfloat16 [128, 8192, 512], P('frame', 'tile'), may hold values from 0 to 0.19921875
- patches: bfloat16 [4096, 64, 64], P('tile'), may hold values from 0.0049743652 to 0.049804688
- patch_rows: int32 [4096], P('tile'), may hold values from -32 to 31
- patch_cols: int32 [4096], P('tile'), may hold values from 0 to 63
- neuron_live: int32 [4096], P('tile'), may hold values from 0 to 1
- neuron_colour: int32 [4096], replicated, may hold values from 0 to 15, as said below
- traces: float32 [4096, 128], P('tile', 'frame'), may hold values from 0.2 to 2
Outputs:
- new_traces: float32 [4096, 128], P('tile', 'frame')
- new_patches: bfloat16 [4096, 64, 64], P('tile')
The draws below stay inside these ranges and needn't reach their ends.
Inputs may be any that keep to these rules, and one draw needn't show every extreme that they name: `neuron_colour`: slots of one colour never share a pixel: within one tile and column bin every slot has its own colour, and the colours of a bin in a tile and in an adjacent tile are disjoint.
All inputs are finite; a program needn't handle non-finite values.
Results may differ from the reference program's by a relative error of at most 0.005.
Values may be sent and summed in bfloat16 or wider, within the bound.
No kernel may reach another device: no remote copies, remote signals or barrier semaphores. Data moves between devices by JAX's collectives and lax.ppermute only.
A program may use at most 64 MiB of HBM per device.

```python
import math
import jax
import jax.numpy as jnp
from jax import lax

PATCH = 64
BINS = 4
LAYERS = 8
SLOTS = 32
COLOURS = 16
NEURONS = 4096
FRAMES = 128
HEIGHT = 8192
WIDTH = 512
N_TILE = 128


def draw_neuron_colour(key, part):
    stream = jax.random.fold_in(key, 7)
    parity_key, ranking_key = jax.random.split(stream)
    tile_total = NEURONS // SLOTS
    parity_shift = jax.random.randint(parity_key, (BINS,), 0, 2)
    tile_ids = jnp.arange(tile_total, dtype=jnp.int32)
    colour_half = (tile_ids[:, None] + parity_shift[None, :]) % 2
    scores = jax.random.randint(ranking_key, (tile_total, BINS, LAYERS), 0, 1 << 20) * LAYERS + jnp.arange(LAYERS, dtype=jnp.int32)
    ranking = jnp.argsort(scores, axis=-1).astype(jnp.int32)
    colour = colour_half[:, :, None] * LAYERS + ranking
    return colour.reshape(NEURONS).astype(jnp.int32)


def slot_roles():
    within = jnp.arange(NEURONS, dtype=jnp.int32) % SLOTS
    return (within == 0, within == 1)


def draw_patch_rows(key, part):
    stream = jax.random.fold_in(key, 11)
    base_key, down_key, up_key = jax.random.split(stream, 3)
    reach_down, reach_up = slot_roles()
    base = jax.random.randint(base_key, (NEURONS,), -(PATCH // 2), PATCH // 2)
    downward = jax.random.randint(down_key, (NEURONS,), PATCH // 4, PATCH // 2)
    upward = jax.random.randint(up_key, (NEURONS,), -(PATCH // 2), -(PATCH // 4))
    picked = jnp.where(reach_down, downward, jnp.where(reach_up, upward, base))
    return picked.astype(jnp.int32)


def draw_patch_cols(key, part):
    stream = jax.random.fold_in(key, 13)
    base_key, centre_key = jax.random.split(stream)
    reach_down, reach_up = slot_roles()
    base = jax.random.randint(base_key, (NEURONS,), 0, PATCH)
    centred = jax.random.randint(centre_key, (NEURONS,), PATCH // 4, 3 * PATCH // 4)
    return jnp.where(reach_down | reach_up, centred, base).astype(jnp.int32)


def draw_neuron_live(key, part):
    stream = jax.random.fold_in(key, 17)
    reach_down, reach_up = slot_roles()
    base = jax.random.randint(stream, (NEURONS,), 0, 2)
    return jnp.where(reach_down | reach_up, 1, base).astype(jnp.int32)


def shard_levels(own_key, extent, shards, low, high):
    loudness = 1.0
    for axis_at, blocks in shards:
        heights = jax.random.uniform(jax.random.fold_in(jax.random.fold_in(own_key, 6), axis_at), (blocks,), jnp.float32, low / len(shards), high / len(shards))
        loudness = loudness * jnp.repeat(jnp.exp(heights), extent[axis_at] // blocks).reshape((-1,) + (1,) * (len(extent) - 1 - axis_at))
    return loudness


def setup_inputs(seed: int = 0) -> dict:
    splits = jax.random.split(jax.random.key(seed), 8)
    movie_block = jnp.clip(0.19921875 * jax.random.uniform(splits[0], (FRAMES, HEIGHT, WIDTH), jnp.float32) ** shard_levels(splits[0], (FRAMES, HEIGHT, WIDTH), ((0, 2), (1, 128)), -0.2, 0.2), 0.0, 0.19921875).astype(jnp.bfloat16)
    patches = jnp.clip(jnp.exp(math.log(0.049804688) - 2.3038113 * jax.random.uniform(splits[1], (NEURONS, PATCH, PATCH), jnp.float32) ** shard_levels(splits[1], (NEURONS, PATCH, PATCH), ((0, 128),), -0.2, 0.2)), 0.0049743652, 0.049804688).astype(jnp.bfloat16)
    patch_rows = draw_patch_rows(jax.random.fold_in(splits[7], 71), 0)
    patch_cols = draw_patch_cols(jax.random.fold_in(splits[7], 71), 0)
    neuron_live = draw_neuron_live(jax.random.fold_in(splits[7], 71), 0)
    neuron_colour = draw_neuron_colour(jax.random.fold_in(splits[7], 71), 0)
    traces = jnp.clip(jnp.exp(math.log(2.0) - 2.3025851 * jax.random.uniform(splits[6], (NEURONS, FRAMES), jnp.float32) ** shard_levels(splits[6], (NEURONS, FRAMES), ((0, 128), (1, 2)), -0.2, 0.2)), 0.2, 2.0)
    return {"movie_block": movie_block, "patches": patches, "patch_rows": patch_rows, "patch_cols": patch_cols, "neuron_live": neuron_live, "neuron_colour": neuron_colour, "traces": traces}


floor_share = 0.25
exact = lax.Precision.HIGHEST


def placement_tables(rows_offset, cols_offset, slab_edge, patch_side):
    slab_lines = jnp.arange(slab_edge, dtype=jnp.int32)
    patch_lines = jnp.arange(patch_side, dtype=jnp.int32)
    half_side = patch_side // 2
    row_pick = slab_lines[None, :, None] == (half_side + rows_offset)[:, None, None] + patch_lines[None, None, :]
    col_pick = patch_lines[None, :, None] + cols_offset[:, None, None] == slab_lines[None, None, :]
    return row_pick, col_pick


def from_before(values):
    return jnp.concatenate([jnp.zeros_like(values[:1]), values[:-1]], axis=0)


def from_after(values):
    return jnp.concatenate([values[1:], jnp.zeros_like(values[:1])], axis=0)


def reference(movie_block, patches, patch_rows, patch_cols, neuron_live, neuron_colour, traces):
    half_side = PATCH // 2
    slab_edge = 2 * PATCH
    row_pick, col_pick = placement_tables(patch_rows, patch_cols, slab_edge, PATCH)
    owners = jnp.arange(NEURONS, dtype=jnp.int32) // SLOTS
    slab_lines = jnp.arange(slab_edge, dtype=jnp.int32)
    image_row = PATCH * owners[:, None] - half_side + slab_lines[None, :]
    inside = (image_row >= 0) & (image_row < HEIGHT)
    row_ok = jnp.any(row_pick, axis=2) & inside & (neuron_live[:, None] > 0)
    col_ok = jnp.any(col_pick, axis=1)
    support = row_ok[:, :, None] & col_ok[:, None, :]
    placed = jnp.einsum("nei,nij->nej", row_pick.astype(jnp.float32), patches.astype(jnp.float32)).astype(jnp.bfloat16)
    spread = jnp.einsum("nej,njc->nec", placed.astype(jnp.float32), col_pick.astype(jnp.float32))
    slabs = jnp.where(support, spread, 0.0).astype(jnp.bfloat16)
    grid_shape = (N_TILE, BINS, LAYERS, slab_edge, slab_edge)
    slab_grid = slabs.reshape(grid_shape)
    support_grid = support.reshape(grid_shape)
    slab_float = slab_grid.astype(jnp.float32)
    gram_own = jnp.einsum("tbnec,tbmec->tbnm", slab_float, slab_float)
    gram_prev = jnp.einsum("tbnec,tbmec->tbnm", slab_float[:, :, :, :PATCH], from_before(slab_float)[:, :, :, PATCH:])
    gram_next = jnp.einsum("tbnec,tbmec->tbnm", slab_float[:, :, :, PATCH:], from_after(slab_float)[:, :, :, :PATCH])
    movie_tiles = movie_block.reshape(FRAMES, N_TILE, PATCH, WIDTH)
    tile_ids = jnp.arange(N_TILE, dtype=jnp.int32)

    def extended_rows(tile_now):
        upper = lax.dynamic_index_in_dim(movie_tiles, jnp.maximum(tile_now - 1, 0), 1, keepdims=False)[:, half_side:]
        middle = lax.dynamic_index_in_dim(movie_tiles, tile_now, 1, keepdims=False)
        lower = lax.dynamic_index_in_dim(movie_tiles, jnp.minimum(tile_now + 1, N_TILE - 1), 1, keepdims=False)[:, :half_side]
        upper = jnp.where(tile_now > 0, upper, jnp.zeros_like(upper))
        lower = jnp.where(tile_now < N_TILE - 1, lower, jnp.zeros_like(lower))
        joined = jnp.concatenate([upper, middle, lower], axis=1)
        return joined.reshape(FRAMES, slab_edge, BINS, slab_edge).astype(jnp.float32)

    def drive_tile(tile_now):
        slab_now = lax.dynamic_index_in_dim(slab_float, tile_now, 0, keepdims=False)
        return jnp.einsum("bnec,febc->bnf", slab_now, extended_rows(tile_now))

    drive = lax.map(drive_tile, tile_ids)
    alive_grid = neuron_live.reshape(N_TILE, BINS, LAYERS).astype(jnp.float32)
    colour_grid = neuron_colour.reshape(N_TILE, BINS, LAYERS)
    denominator = jnp.diagonal(gram_own, axis1=2, axis2=3) + (1.0 - alive_grid)

    def temporal_step(colour_now, current):
        coupled = jnp.einsum("tbnm,tbmf->tbnf", gram_own, current, precision=exact)
        coupled = coupled + jnp.einsum("tbnm,tbmf->tbnf", gram_prev, from_before(current), precision=exact)
        coupled = coupled + jnp.einsum("tbnm,tbmf->tbnf", gram_next, from_after(current), precision=exact)
        proposal = jnp.maximum(current + (drive - coupled) / denominator[..., None], 0.0)
        return jnp.where((colour_grid == colour_now)[..., None], proposal, current)

    start = traces.reshape(N_TILE, BINS, LAYERS, FRAMES) * alive_grid[..., None]
    settled = lax.fori_loop(0, COLOURS, temporal_step, start)
    rounded = settled.astype(jnp.bfloat16)

    def field_tile(tile_now):
        trace_now = lax.dynamic_index_in_dim(rounded, tile_now, 0, keepdims=False).astype(jnp.float32)
        return jnp.einsum("febc,bnf->bnec", extended_rows(tile_now), trace_now)

    field = lax.map(field_tile, tile_ids)
    cross_own = jnp.einsum("tbnf,tbmf->tbnm", settled, settled, precision=exact)
    cross_prev = jnp.einsum("tbnf,tbmf->tbnm", settled, from_before(settled), precision=exact)
    cross_next = jnp.einsum("tbnf,tbmf->tbnm", settled, from_after(settled), precision=exact)
    spatial_den = jnp.maximum(jnp.diagonal(cross_own, axis1=2, axis2=3), floor_share * FRAMES)

    def spatial_step(colour_now, state):
        state_float = state.astype(jnp.float32)
        upper = from_before(state_float)[:, :, :, PATCH:]
        lower = from_after(state_float)[:, :, :, :PATCH]
        top = jnp.einsum("tbnm,tbmec->tbnec", cross_own, state_float[:, :, :, :PATCH], precision=exact)
        top = top + jnp.einsum("tbnm,tbmec->tbnec", cross_prev, upper, precision=exact)
        bottom = jnp.einsum("tbnm,tbmec->tbnec", cross_own, state_float[:, :, :, PATCH:], precision=exact)
        bottom = bottom + jnp.einsum("tbnm,tbmec->tbnec", cross_next, lower, precision=exact)
        mixed = jnp.concatenate([top, bottom], axis=3)
        proposal = jnp.maximum(state_float + (field - mixed) / spatial_den[..., None, None], 0.0)
        chosen = (colour_grid == colour_now)[..., None, None]
        return jnp.where(chosen, jnp.where(support_grid, proposal, 0.0), state_float).astype(jnp.bfloat16)

    final = lax.fori_loop(0, COLOURS, spatial_step, slab_grid)
    final_flat = final.reshape(NEURONS, slab_edge, slab_edge).astype(jnp.float32)
    lifted = jnp.einsum("nei,nec->nic", row_pick.astype(jnp.float32), final_flat).astype(jnp.bfloat16)
    new_patches = jnp.einsum("nic,njc->nij", lifted.astype(jnp.float32), col_pick.astype(jnp.float32)).astype(jnp.bfloat16)
    return settled.reshape(NEURONS, FRAMES), new_patches
```

```python
import functools

import jax
import jax.numpy as jnp
from jax import lax
from jax.experimental import pallas as pl
from jax.experimental.pallas import tpu as pltpu
from jax.sharding import PartitionSpec as P

exact = lax.Precision.HIGHEST
f32 = jnp.float32
bf16 = jnp.bfloat16
BINS = 4
LAYERS = 8
SLOTS = 32
COLOURS = 16
PATCH = 64
HALF = 32
EDGE = 128
FRAMES = 128
GROUP = BINS * COLOURS
floor_share = 0.25

vmem = pl.BlockSpec(memory_space=pltpu.VMEM)
smem = pl.BlockSpec(memory_space=pltpu.SMEM)


def iota(shape, dim):
    return lax.broadcasted_iota(jnp.int32, shape, dim)


def dot_nt(a, b, precision=None):
    return lax.dot_general(
        a, b, (((1,), (1,)), ((), ())), precision=precision, preferred_element_type=f32
    )


def dot(a, b, precision=None):
    return lax.dot_general(
        a, b, (((1,), (0,)), ((), ())), precision=precision, preferred_element_type=f32
    )


def neighbour_tile(tile, core, tiles):
    other = jnp.where(core == 0, tile - 1, tile + 1)
    other = jnp.where(other < 0, tile + 1, other)
    return jnp.where(other >= tiles, tile - 1, other)


def slab_kernel(rows_ref, cols_ref, live_ref, patches_ref, out_ref, own_ref):
    core = lax.axis_index("frame")
    line = iota((PATCH, PATCH), 0)
    base_out = jnp.where(core == 0, 0, 96)
    base_own = jnp.where(core == 0, 32, 64)
    row_at = jnp.where(line < HALF, base_out + line, base_own + line - HALF) - HALF
    row_at = row_at - iota((PATCH, PATCH), 1)
    col_at = iota((PATCH, EDGE), 1) - iota((PATCH, EDGE), 0)
    for s in range(SLOTS):
        live = live_ref[s] > 0
        row_pick = jnp.where((row_at == rows_ref[s]) & live, 1.0, 0.0).astype(bf16)
        col_pick = jnp.where(col_at == cols_ref[s], 1.0, 0.0).astype(bf16)
        placed = dot(row_pick, patches_ref[s]).astype(bf16)
        spread = dot(placed, col_pick).astype(bf16)
        out_ref[s] = spread[:HALF]
        own_ref[s] = spread[HALF:]


def partial_kernel(
    tiles, core_ref, colour_ref, live_ref, mine_ref, other_ref, own_ref, recv_ref,
    near_ref, far_ref, slab_ref, message_ref, live_rows_ref,
):
    tile = lax.axis_index("tile")
    core = lax.axis_index("frame")
    beside = neighbour_tile(tile, core, tiles)
    message_ref[...] = jnp.zeros_like(message_ref)
    live_rows_ref[...] = jnp.zeros_like(live_rows_ref)
    start = GROUP + COLOURS
    wide = jnp.concatenate([near_ref[...], far_ref[...]], axis=1)
    swapped = jnp.concatenate([far_ref[...], near_ref[...]], axis=1)
    first = jnp.where(core == 0, wide, swapped)
    for s in range(SLOTS):
        b = s // LAYERS
        mine = b * COLOURS + colour_ref[tile * SLOTS + s]
        theirs = b * COLOURS + colour_ref[beside * SLOTS + s]
        slab_ref[mine] = own_ref[s]
        slab_ref[theirs] = recv_ref[s]
        alive = live_ref[s].astype(f32)
        message_ref[pl.ds(start + mine, 1), :] = first[s : s + 1] * alive
        live_rows_ref[pl.ds(mine, 1), :] = jnp.full((1, FRAMES), alive, f32)
    same_row = iota((1024, 256), 0) % 16 == iota((1024, 256), 1) % 16
    fold = jnp.where(iota((COLOURS, 256), 1) // 16 == iota((COLOURS, 256), 0), 1.0, 0.0)
    gram = jnp.zeros((COLOURS, EDGE), f32)
    for b in range(BINS):
        lanes = slice(b * EDGE, (b + 1) * EDGE)
        both = [
            slab_ref[b * COLOURS : (b + 1) * COLOURS, 16 * q : 16 * q + 16, :].reshape(256, EDGE)
            for q in range(2)
        ]
        both = jnp.concatenate(both, axis=1)
        parts = []
        for ref in (mine_ref, other_ref):
            pixels = [ref[:, 16 * q : 16 * q + 16, lanes].reshape(1024, EDGE) for q in range(2)]
            pixels = jnp.concatenate(pixels, axis=1)
            product = jnp.where(same_row, dot_nt(pixels, both), 0.0)
            parts.append(jnp.sum(product.reshape(64, 16, 256), axis=1))
        near = jnp.concatenate(parts, axis=0)
        far = jnp.concatenate(parts[::-1], axis=0)
        ordered = jnp.where(core == 0, near, far)
        message_ref[b * COLOURS : (b + 1) * COLOURS, :] = dot_nt(fold, ordered, exact)
        square = jnp.where(same_row[:256], dot_nt(both, both), 0.0)
        square = jnp.sum(square.reshape(COLOURS, 16, 256), axis=1)
        spread = iota((256, EDGE), 0) // 16 + b * COLOURS == iota((256, EDGE), 1)
        gram = gram + dot(square, jnp.where(spread, 1.0, 0.0), exact)
    message_ref[GROUP : GROUP + COLOURS, :] = gram


def block_diagonal(gram):
    tall = jnp.concatenate([gram] * BINS, axis=0)[:, :GROUP]
    keep = iota((GROUP, GROUP), 0) // COLOURS == iota((GROUP, GROUP), 1) // COLOURS
    return jnp.where(keep, tall, 0.0)


def join_kernel(mine_ref, pair_ref, out_ref, start_ref):
    grams = slice(GROUP, GROUP + COLOURS)
    traces = slice(GROUP + COLOURS, 2 * GROUP + COLOURS)
    gram = mine_ref[grams, :] + pair_ref[grams, :]
    current = mine_ref[traces, :] + pair_ref[traces, :]
    drive = mine_ref[:GROUP, :] + pair_ref[:GROUP, :]
    out_ref[:GROUP, :] = drive - dot(block_diagonal(gram), current, exact)
    out_ref[grams, :] = gram
    start_ref[...] = mine_ref[traces, :]


def settle(phase_ref, live_ref, gram, residual, current, phase, state_ref, change_ref):
    whole = jnp.concatenate([gram] * BINS, axis=0)
    lane = iota((GROUP, EDGE), 1)
    diag = jnp.sum(jnp.where(lane == iota((GROUP, EDGE), 0), whole, 0.0), axis=1, keepdims=True)
    inverse = 1.0 / (diag + (1.0 - live_ref[...]))
    chosen = phase_ref[...] == phase
    news = []
    changes = []
    for b in range(BINS):
        rows = slice(b * COLOURS, (b + 1) * COLOURS)
        rest, now = residual[rows], current[rows]
        inv, pick = inverse[rows], chosen[rows]
        row_id = iota((COLOURS, FRAMES), 0)
        change = jnp.zeros((COLOURS, FRAMES), f32)
        for g in range(COLOURS):
            at = slice(g, g + 1)
            value = jnp.maximum(now[at] + rest[at] * inv[at], 0.0) - now[at]
            delta = jnp.where(pick[at], value, 0.0)
            lane_at = slice(b * COLOURS + g, b * COLOURS + g + 1)
            column = jnp.broadcast_to(gram[:, lane_at], (COLOURS, FRAMES))
            rest = rest - column * delta
            change = jnp.where(row_id == g, delta, change)
        state_ref[rows, :] = rest
        state_ref[GROUP + b * COLOURS : GROUP + (b + 1) * COLOURS, :] = now + change
        change_ref[rows, :] = change


def first_phase_kernel(phase_ref, live_ref, start_ref, here_ref, there_ref, state_ref, change_ref):
    grams = slice(GROUP, GROUP + COLOURS)
    gram = here_ref[grams, :] + there_ref[grams, :]
    residual = here_ref[:GROUP, :] + there_ref[:GROUP, :]
    settle(phase_ref, live_ref, gram, residual, start_ref[...], 0, state_ref, change_ref)


def relay_kernel(here_ref, delta_ref, out_ref):
    grams = slice(GROUP, GROUP + COLOURS)
    out_ref[...] = dot(block_diagonal(here_ref[grams, :]), delta_ref[...], exact)


def next_phase_kernel(
    step_ref, phase_ref, live_ref, here_ref, there_ref, mine_ref, other_ref, old_ref, beside_ref,
    delta_ref, state_ref, change_ref, beside_out_ref,
):
    grams = slice(GROUP, GROUP + COLOURS)
    gram = here_ref[grams, :] + there_ref[grams, :]
    residual = old_ref[:GROUP, :] - (mine_ref[...] + other_ref[...])
    current = old_ref[GROUP:, :]
    beside_out_ref[...] = beside_ref[...] + delta_ref[...]
    settle(phase_ref, live_ref, gram, residual, current, step_ref[0], state_ref, change_ref)


def spatial_kernel(
    tiles, core_ref, colour_ref, mine_ref, other_ref, slab_ref, state_in_ref, beside_ref, delta_ref,
    traces_ref, out_ref, own_ref, weight_ref, cross_ref, field_ref, state_ref,
):
    tile = lax.axis_index("tile")
    core = lax.axis_index("frame")
    beside = neighbour_tile(tile, core, tiles)
    own = state_in_ref[GROUP:, :]
    rolled = jnp.concatenate([own[:, 64:], own[:, :64]], axis=1)
    framed = jnp.where(core == 0, own, rolled)[:, :64]
    cross_ref[:GROUP, :64] = framed
    for s in range(SLOTS):
        at = (s // LAYERS) * COLOURS + colour_ref[tile * SLOTS + s]
        traces_ref[s : s + 1, :] = cross_ref[pl.ds(at, 1), :64]
    both = own + beside_ref[...] + delta_ref[...]
    position = (iota((FRAMES, 2048), 1) // 16 + 64 * core) % FRAMES
    repeat = jnp.where(position == iota((FRAMES, 2048), 0), 1.0, 0.0).astype(bf16)
    repeated = dot(both.astype(bf16), repeat)
    same_row = iota((16, 2048), 0) == iota((16, 2048), 1) % 16
    for b in range(BINS):
        rows = slice(b * COLOURS, (b + 1) * COLOURS)
        lanes = slice(b * EDGE, (b + 1) * EDGE)
        for g in range(COLOURS):
            line = repeated[b * COLOURS + g : b * COLOURS + g + 1]
            weight_ref[16 * g : 16 * g + 16, :] = jnp.where(same_row, line, 0.0).astype(bf16)
        pixels = []
        for ref in (mine_ref, other_ref):
            part = [ref[:, 16 * q : 16 * q + 16, lanes].reshape(1024, EDGE) for q in range(2)]
            pixels.append(jnp.concatenate(part, axis=1))
        field_ref[b] = dot(weight_ref[...], jnp.concatenate(pixels, axis=0))
        now = both[rows]
        cross = dot_nt(now, now, exact)
        for g in range(COLOURS):
            column = jnp.broadcast_to(cross[:, g : g + 1], (COLOURS, EDGE))
            cross_ref[(b * COLOURS + g) * 16 : (b * COLOURS + g) * 16 + 16, :] = column

    floor = floor_share * FRAMES

    def update(step, carry):
        b = step // 2
        q = step % 2
        first = b * COLOURS
        row = pl.multiple_of(q * 16, 16)
        states = [
            slab_ref[first + m, pl.ds(row, 16), :].astype(f32) for m in range(COLOURS)
        ]
        for g in range(COLOURS):
            base = (first + g) * 16
            support = states[g] > 0.0
            mixed = jnp.zeros((16, EDGE), f32)
            for m in range(COLOURS):
                mixed = mixed + cross_ref[pl.ds(base + m, 1), :] * states[m]
            scale = 1.0 / jnp.maximum(cross_ref[pl.ds(base + g, 1), :], floor)
            lane = pl.multiple_of(q * EDGE, EDGE)
            field = field_ref[b, 16 * g : 16 * g + 16, pl.ds(lane, EDGE)]
            fresh = jnp.maximum(states[g] + (field - mixed) * scale, 0.0)
            fresh = jnp.where(support, fresh, 0.0).astype(bf16)
            state_ref[first + g, pl.ds(row, 16), :] = fresh
            states[g] = fresh.astype(f32)
        return carry

    lax.fori_loop(0, 2 * BINS, update, 0)
    for s in range(SLOTS):
        first = (s // LAYERS) * COLOURS
        own_ref[s] = state_ref[first + colour_ref[tile * SLOTS + s]]
        out_ref[s] = state_ref[first + colour_ref[beside * SLOTS + s]]


def patch_kernel(rows_ref, cols_ref, own_ref, recv_ref, sib_own_ref, sib_recv_ref, out_ref):
    core = lax.axis_index("frame")
    line = iota((PATCH, EDGE), 1)
    block = line // HALF
    home = jnp.where(core == 0, HALF, 2 * HALF)
    edge = jnp.where(core == 0, 0, 3 * HALF)
    far_home = 3 * HALF - home
    far_edge = 3 * HALF - edge
    base = jnp.where(block == 0, home, jnp.where(block == 1, edge, jnp.where(block == 2, far_home, far_edge)))
    row_at = base + line % HALF - HALF - iota((PATCH, EDGE), 0)
    col_at = iota((EDGE, PATCH), 0) - iota((EDGE, PATCH), 1)
    for s in range(SLOTS):
        row_pick = jnp.where(row_at == rows_ref[s], 1.0, 0.0).astype(bf16)
        col_pick = jnp.where(col_at == cols_ref[s], 1.0, 0.0).astype(bf16)
        whole = jnp.concatenate([own_ref[s], recv_ref[s], sib_own_ref[s], sib_recv_ref[s]], axis=0)
        lifted = dot(row_pick, whole).astype(bf16)
        out_ref[s] = dot(lifted, col_pick).astype(bf16)


def shape(dims, dtype=f32):
    return jax.ShapeDtypeStruct(dims, dtype)


def call(kernel, ins, outs, name, scratch=(), limit=None):
    return pl.pallas_call(
        kernel,
        in_specs=ins,
        out_specs=[vmem] * len(outs),
        out_shape=outs,
        scratch_shapes=list(scratch),
        name=name,
        compiler_params=pltpu.CompilerParams(vmem_limit_bytes=limit) if limit else None,
    )


def on_device(movie_block, patches, patch_rows, patch_cols, neuron_live, neuron_colour, traces):
    tiles = lax.axis_size("tile")
    core = lax.axis_index("frame")
    tile = lax.axis_index("tile")
    swap_pairs = []
    for t in range(tiles - 1):
        swap_pairs += [(2 * t + 1, 2 * t + 2), (2 * t + 2, 2 * t + 1)]

    def pair_swap(value):
        return lax.ppermute(value, ("tile", "frame"), swap_pairs)

    def chip_swap(value):
        return lax.ppermute(value, "frame", [(0, 1), (1, 0)])

    own_colour = lax.dynamic_slice_in_dim(neuron_colour, tile * SLOTS, SLOTS)
    owned = jnp.any(
        own_colour.reshape(BINS, LAYERS, 1) == jnp.arange(COLOURS, dtype=jnp.int32), axis=1
    )
    turns = (owned[:, 1:] != owned[:, :-1]).astype(jnp.int32)
    later = jnp.arange(COLOURS)[None, :] > jnp.arange(COLOURS - 1)[:, None]
    phase_of = jnp.sum(jnp.where(later[None], turns[:, :, None], 0), axis=1)
    phase_count = jnp.max(jnp.sum(turns, axis=1)) + 1
    phases = jnp.where(owned, phase_of, -1).reshape(GROUP, 1)
    phases = jnp.broadcast_to(phases, (GROUP, FRAMES))

    movie_out = lax.dynamic_slice_in_dim(movie_block, HALF * (1 - core), HALF, 1)
    movie_other = chip_swap(movie_out)
    traces_other = chip_swap(traces)

    piece_out, piece_own = call(
        slab_kernel,
        [smem, smem, smem, vmem],
        [shape((SLOTS, HALF, EDGE), bf16)] * 2,
        "slabs",
    )(patch_rows, patch_cols, neuron_live, patches)
    piece_recv = pair_swap(piece_out)

    core_at = core.reshape(1)
    movie_spec = pl.BlockSpec((64, HALF, 512), lambda i, c: (0, c[0], 0))
    whole2 = lambda dims: pl.BlockSpec(dims, lambda i, c: (0,) * len(dims))
    smem_in = pl.BlockSpec(memory_space=pltpu.SMEM)

    slab, message, live_rows = pl.pallas_call(
        functools.partial(partial_kernel, tiles),
        grid_spec=pltpu.PrefetchScalarGridSpec(
            num_scalar_prefetch=1,
            grid=(1,),
            in_specs=[
                smem_in, smem_in, movie_spec, whole2((64, HALF, 512)), whole2((SLOTS, HALF, EDGE)),
                whole2((SLOTS, HALF, EDGE)), whole2((SLOTS, 64)), whole2((SLOTS, 64)),
            ],
            out_specs=[
                whole2((GROUP, HALF, EDGE)), whole2((2 * GROUP + COLOURS, FRAMES)),
                whole2((GROUP, FRAMES)),
            ],
        ),
        out_shape=[
            shape((GROUP, HALF, EDGE), bf16), shape((2 * GROUP + COLOURS, FRAMES)),
            shape((GROUP, FRAMES)),
        ],
        compiler_params=pltpu.CompilerParams(vmem_limit_bytes=40 * 2**20),
        name="partial_sums",
    )(
        core_at, neuron_colour, neuron_live, movie_block, movie_other, piece_own, piece_recv,
        traces, traces_other,
    )

    message_pair = pair_swap(message)
    here, start = call(
        join_kernel, [vmem] * 2, [shape((GROUP + COLOURS, FRAMES)), shape((GROUP, FRAMES))], "join"
    )(message, message_pair)
    there = chip_swap(here)
    beside = message_pair[GROUP + COLOURS :]
    state_shapes = [shape((2 * GROUP, FRAMES)), shape((GROUP, FRAMES))]
    state, change = call(first_phase_kernel, [vmem] * 5, state_shapes, "first_phase")(
        phases, live_rows, start, here, there
    )

    def advance(carry):
        step, state, beside, change = carry
        delta = pair_swap(change)
        (mine,) = call(relay_kernel, [vmem] * 2, [shape((GROUP, FRAMES))], "relay")(here, delta)
        other = chip_swap(mine)
        state, change, beside = call(
            next_phase_kernel, [smem] + [vmem] * 9, state_shapes + [shape((GROUP, FRAMES))], "next_phase"
        )(step.reshape(1), phases, live_rows, here, there, mine, other, state, beside, delta)
        return step + 1, state, beside, change

    carry = advance((jnp.int32(1), state, beside, change))
    _, state, beside, change = lax.while_loop(lambda c: c[0] < phase_count, advance, carry)
    delta = pair_swap(change)

    new_traces, final_out, final_own = pl.pallas_call(
        functools.partial(spatial_kernel, tiles),
        grid_spec=pltpu.PrefetchScalarGridSpec(
            num_scalar_prefetch=1,
            grid=(1,),
            in_specs=[
                smem_in, movie_spec, whole2((64, HALF, 512)), whole2((GROUP, HALF, EDGE)),
                whole2((2 * GROUP, FRAMES)), whole2((GROUP, FRAMES)), whole2((GROUP, FRAMES)),
            ],
            out_specs=[whole2((SLOTS, 64)), whole2((SLOTS, HALF, EDGE)), whole2((SLOTS, HALF, EDGE))],
            scratch_shapes=[
                pltpu.VMEM((256, 2048), bf16),
                pltpu.VMEM((GROUP * COLOURS, EDGE), f32),
                pltpu.VMEM((BINS, 256, 256), f32),
                pltpu.VMEM((GROUP, HALF, EDGE), bf16),
            ],
        ),
        out_shape=[
            shape((SLOTS, 64)), shape((SLOTS, HALF, EDGE), bf16), shape((SLOTS, HALF, EDGE), bf16)
        ],
        compiler_params=pltpu.CompilerParams(vmem_limit_bytes=40 * 2**20),
        name="spatial",
    )(core_at, neuron_colour, movie_block, movie_other, slab, state, beside, delta)

    far_own = chip_swap(final_own)
    final_recv = pair_swap(final_out)
    far_recv = chip_swap(final_recv)
    (new_patches,) = call(
        patch_kernel, [smem, smem] + [vmem] * 4, [shape((SLOTS, PATCH, PATCH), bf16)], "patches"
    )(patch_rows, patch_cols, final_own, final_recv, far_own, far_recv)
    return (new_traces, new_patches)


def solution(mesh):
    placed = (
        P("frame", "tile", None),
        P("tile", None, None),
        P("tile"),
        P("tile"),
        P("tile"),
        P(),
        P("tile", "frame"),
    )
    return jax.shard_map(
        on_device,
        mesh=mesh,
        in_specs=placed,
        out_specs=(P("tile", "frame"), P("tile", None, None)),
        check_vma=False,
    )
```

```python
import functools

import jax
import jax.numpy as jnp
from jax import lax
from jax.experimental import pallas as pl
from jax.experimental.pallas import tpu as pltpu
from jax.sharding import PartitionSpec as P

exact = lax.Precision.HIGHEST
f32 = jnp.float32
bf16 = jnp.bfloat16
BINS = 4
LAYERS = 8
SLOTS = 32
COLOURS = 16
PATCH = 64
HALF = 32
EDGE = 128
FRAMES = 128
GROUP = BINS * COLOURS
floor_share = 0.25

vmem = pl.BlockSpec(memory_space=pltpu.VMEM)
smem = pl.BlockSpec(memory_space=pltpu.SMEM)


def iota(shape, dim):
    return lax.broadcasted_iota(jnp.int32, shape, dim)


def dot_nt(a, b, precision=None):
    return lax.dot_general(
        a, b, (((1,), (1,)), ((), ())), precision=precision, preferred_element_type=f32
    )


def dot(a, b, precision=None):
    return lax.dot_general(
        a, b, (((1,), (0,)), ((), ())), precision=precision, preferred_element_type=f32
    )


def neighbour_tile(tile, core, tiles):
    other = jnp.where(core == 0, tile - 1, tile + 1)
    other = jnp.where(other < 0, tile + 1, other)
    return jnp.where(other >= tiles, tile - 1, other)


def slab_kernel(
    rows_ref, cols_ref, live_ref, patches_ref, movie_ref, out_ref, own_ref, keep_ref, send_ref, sems,
):
    core = lax.axis_index("frame")
    sends = pltpu.make_async_copy(
        movie_ref.at[:, pl.ds(pl.multiple_of(HALF * (1 - core), HALF), HALF), :], send_ref, sems.at[0]
    )
    keeps = pltpu.make_async_copy(
        movie_ref.at[:, pl.ds(pl.multiple_of(HALF * core, HALF), HALF), :], keep_ref, sems.at[1]
    )
    sends.start()
    keeps.start()
    line = iota((PATCH, PATCH), 0)
    base_out = jnp.where(core == 0, 0, 96)
    base_own = jnp.where(core == 0, 32, 64)
    row_at = jnp.where(line < HALF, base_out + line, base_own + line - HALF) - HALF
    row_at = row_at - iota((PATCH, PATCH), 1)
    col_at = iota((PATCH, EDGE), 1) - iota((PATCH, EDGE), 0)
    for s in range(SLOTS):
        live = live_ref[s] > 0
        row_pick = jnp.where((row_at == rows_ref[s]) & live, 1.0, 0.0).astype(bf16)
        col_pick = jnp.where(col_at == cols_ref[s], 1.0, 0.0).astype(bf16)
        placed = dot(row_pick, patches_ref[s]).astype(bf16)
        spread = dot(placed, col_pick).astype(bf16)
        out_ref[s] = spread[:HALF]
        own_ref[s] = spread[HALF:]
    sends.wait()
    keeps.wait()


def table_kernel(
    colour_ref, live_ref, traces_ref, phase_ref, live_rows_ref, begin_ref, count_ref, owner_ref
):
    tile = lax.axis_index("tile")
    live_rows_ref[...] = jnp.zeros_like(live_rows_ref)
    for i in range(GROUP):
        owner_ref[i] = 0
    for s in range(SLOTS):
        at = (s // LAYERS) * COLOURS + colour_ref[tile * SLOTS + s]
        owner_ref[at] = 1
        alive = live_ref[s].astype(f32)
        live_rows_ref[pl.ds(at, 1), :] = jnp.full((1, FRAMES), alive, f32)
        begin_ref[s : s + 1, :] = traces_ref[s : s + 1, :] * alive
    most = jnp.int32(0)
    for b in range(BINS):
        phase = jnp.int32(0)
        for g in range(COLOURS):
            i = b * COLOURS + g
            if g:
                phase = phase + jnp.abs(owner_ref[i] - owner_ref[i - 1])
            value = jnp.where(owner_ref[i] == 1, phase, -1)
            phase_ref[i : i + 1, :] = jnp.full((1, FRAMES), value, jnp.int32)
        most = jnp.maximum(most, phase + 1)
    count_ref[0] = most


def partial_kernel(
    tiles, colour_ref, mine_ref, other_ref, own_ref, recv_ref, near_ref, far_ref,
    slab_ref, message_ref,
):
    tile = lax.axis_index("tile")
    core = lax.axis_index("frame")
    beside = neighbour_tile(tile, core, tiles)
    message_ref[...] = jnp.zeros_like(message_ref)
    start = GROUP + COLOURS
    wide = jnp.concatenate([near_ref[...], far_ref[...]], axis=1)
    swapped = jnp.concatenate([far_ref[...], near_ref[...]], axis=1)
    first = jnp.where(core == 0, wide, swapped)
    for s in range(SLOTS):
        b = s // LAYERS
        mine = b * COLOURS + colour_ref[tile * SLOTS + s]
        theirs = b * COLOURS + colour_ref[beside * SLOTS + s]
        slab_ref[mine] = own_ref[s]
        slab_ref[theirs] = recv_ref[s]
        message_ref[pl.ds(start + mine, 1), :] = first[s : s + 1]
    same_row = iota((1024, 256), 0) % 16 == iota((1024, 256), 1) % 16
    fold = jnp.where(iota((COLOURS, 256), 1) // 16 == iota((COLOURS, 256), 0), 1.0, 0.0)
    gram = jnp.zeros((COLOURS, EDGE), f32)
    for b in range(BINS):
        lanes = slice(b * EDGE, (b + 1) * EDGE)
        both = [
            slab_ref[b * COLOURS : (b + 1) * COLOURS, 16 * q : 16 * q + 16, :].reshape(256, EDGE)
            for q in range(2)
        ]
        both = jnp.concatenate(both, axis=1)
        parts = []
        for ref in (mine_ref, other_ref):
            pixels = [ref[:, 16 * q : 16 * q + 16, lanes].reshape(1024, EDGE) for q in range(2)]
            pixels = jnp.concatenate(pixels, axis=1)
            product = jnp.where(same_row, dot_nt(pixels, both), 0.0)
            parts.append(jnp.sum(product.reshape(64, 16, 256), axis=1))
        near = jnp.concatenate(parts, axis=0)
        far = jnp.concatenate(parts[::-1], axis=0)
        ordered = jnp.where(core == 0, near, far)
        message_ref[b * COLOURS : (b + 1) * COLOURS, :] = dot_nt(fold, ordered, exact)
        square = jnp.where(same_row[:256], dot_nt(both, both), 0.0)
        square = jnp.sum(square.reshape(COLOURS, 16, 256), axis=1)
        spread = iota((256, EDGE), 0) // 16 + b * COLOURS == iota((256, EDGE), 1)
        gram = gram + dot(square, jnp.where(spread, 1.0, 0.0), exact)
    message_ref[GROUP : GROUP + COLOURS, :] = gram


def block_diagonal(gram):
    tall = jnp.concatenate([gram] * BINS, axis=0)[:, :GROUP]
    keep = iota((GROUP, GROUP), 0) // COLOURS == iota((GROUP, GROUP), 1) // COLOURS
    return jnp.where(keep, tall, 0.0)


def settle(phase_ref, live_ref, gram, residual, current, phase, state_ref, change_ref):
    whole = jnp.concatenate([gram] * BINS, axis=0)
    lane = iota((GROUP, EDGE), 1)
    diag = jnp.sum(jnp.where(lane == iota((GROUP, EDGE), 0), whole, 0.0), axis=1, keepdims=True)
    inverse = 1.0 / (diag + (1.0 - live_ref[...]))
    chosen = phase_ref[...] == phase
    news = []
    changes = []
    for b in range(BINS):
        rows = slice(b * COLOURS, (b + 1) * COLOURS)
        rest, now = residual[rows], current[rows]
        inv, pick = inverse[rows], chosen[rows]
        row_id = iota((COLOURS, FRAMES), 0)
        change = jnp.zeros((COLOURS, FRAMES), f32)
        for g in range(COLOURS):
            at = slice(g, g + 1)
            value = jnp.maximum(now[at] + rest[at] * inv[at], 0.0) - now[at]
            delta = jnp.where(pick[at], value, 0.0)
            lane_at = slice(b * COLOURS + g, b * COLOURS + g + 1)
            column = jnp.broadcast_to(gram[:, lane_at], (COLOURS, FRAMES))
            rest = rest - column * delta
            change = jnp.where(row_id == g, delta, change)
        state_ref[rows, :] = rest
        state_ref[GROUP + b * COLOURS : GROUP + (b + 1) * COLOURS, :] = now + change
        change_ref[rows, :] = change


def first_phase_kernel(
    phase_ref, live_ref, mine_ref, pair_ref, far_ref, far_pair_ref,
    state_ref, change_ref, gram_ref, beside_ref,
):
    drives = slice(0, GROUP)
    grams = slice(GROUP, GROUP + COLOURS)
    traces = slice(GROUP + COLOURS, 2 * GROUP + COLOURS)
    here = mine_ref[grams, :] + pair_ref[grams, :]
    there = far_ref[grams, :] + far_pair_ref[grams, :]
    drive = mine_ref[drives, :] + pair_ref[drives, :] + far_ref[drives, :] + far_pair_ref[drives, :]
    start = mine_ref[traces, :]
    coupled = dot(block_diagonal(here + there), start, exact)
    coupled = coupled + dot(block_diagonal(here), pair_ref[traces, :], exact)
    coupled = coupled + dot(block_diagonal(there), far_pair_ref[traces, :], exact)
    gram_ref[:COLOURS, :] = here
    gram_ref[COLOURS:, :] = there
    beside_ref[...] = pair_ref[traces, :]
    settle(phase_ref, live_ref, here + there, drive - coupled, start, 0, state_ref, change_ref)


def next_phase_kernel(
    step_ref, phase_ref, live_ref, gram_ref, old_ref, beside_ref, delta_ref, far_delta_ref,
    state_ref, change_ref, beside_out_ref,
):
    here = gram_ref[:COLOURS, :]
    there = gram_ref[COLOURS:, :]
    coupled = dot(block_diagonal(here), delta_ref[...], exact)
    coupled = coupled + dot(block_diagonal(there), far_delta_ref[...], exact)
    residual = old_ref[:GROUP, :] - coupled
    beside_out_ref[...] = beside_ref[...] + delta_ref[...]
    settle(
        phase_ref, live_ref, here + there, residual, old_ref[GROUP:, :], step_ref[0],
        state_ref, change_ref,
    )


def spatial_kernel(
    tiles, colour_ref, mine_ref, other_ref, slab_ref, state_in_ref, beside_ref, delta_ref,
    traces_ref, out_ref, own_ref, weight_ref, cross_ref, field_ref, state_ref, far_ref, sem,
):
    fetch = pltpu.make_async_copy(other_ref, far_ref, sem)
    fetch.start()
    tile = lax.axis_index("tile")
    core = lax.axis_index("frame")
    beside = neighbour_tile(tile, core, tiles)
    own = state_in_ref[GROUP:, :]
    rolled = jnp.concatenate([own[:, 64:], own[:, :64]], axis=1)
    framed = jnp.where(core == 0, own, rolled)[:, :64]
    cross_ref[:GROUP, :64] = framed
    for s in range(SLOTS):
        at = (s // LAYERS) * COLOURS + colour_ref[tile * SLOTS + s]
        traces_ref[s : s + 1, :] = cross_ref[pl.ds(at, 1), :64]
    both = own + beside_ref[...] + delta_ref[...]
    position = (iota((FRAMES, 2048), 1) // 16 + 64 * core) % FRAMES
    repeat = jnp.where(position == iota((FRAMES, 2048), 0), 1.0, 0.0).astype(bf16)
    repeated = dot(both.astype(bf16), repeat)
    same_row = iota((16, 2048), 0) == iota((16, 2048), 1) % 16
    fetch.wait()
    for b in range(BINS):
        rows = slice(b * COLOURS, (b + 1) * COLOURS)
        lanes = slice(b * EDGE, (b + 1) * EDGE)
        for g in range(COLOURS):
            line = repeated[b * COLOURS + g : b * COLOURS + g + 1]
            weight_ref[16 * g : 16 * g + 16, :] = jnp.where(same_row, line, 0.0).astype(bf16)
        pixels = []
        for ref in (mine_ref, far_ref):
            part = [ref[:, 16 * q : 16 * q + 16, lanes].reshape(1024, EDGE) for q in range(2)]
            pixels.append(jnp.concatenate(part, axis=1))
        field_ref[b] = dot(weight_ref[...], jnp.concatenate(pixels, axis=0))
        now = both[rows]
        cross = dot_nt(now, now, exact)
        for g in range(COLOURS):
            column = jnp.broadcast_to(cross[:, g : g + 1], (COLOURS, EDGE))
            cross_ref[(b * COLOURS + g) * 16 : (b * COLOURS + g) * 16 + 16, :] = column

    floor = floor_share * FRAMES

    def update(step, carry):
        b = step // 2
        q = step % 2
        first = b * COLOURS
        row = pl.multiple_of(q * 16, 16)
        states = [
            slab_ref[first + m, pl.ds(row, 16), :].astype(f32) for m in range(COLOURS)
        ]
        for g in range(COLOURS):
            base = (first + g) * 16
            support = states[g] > 0.0
            mixed = jnp.zeros((16, EDGE), f32)
            for m in range(COLOURS):
                mixed = mixed + cross_ref[pl.ds(base + m, 1), :] * states[m]
            scale = 1.0 / jnp.maximum(cross_ref[pl.ds(base + g, 1), :], floor)
            lane = pl.multiple_of(q * EDGE, EDGE)
            field = field_ref[b, 16 * g : 16 * g + 16, pl.ds(lane, EDGE)]
            fresh = jnp.maximum(states[g] + (field - mixed) * scale, 0.0)
            fresh = jnp.where(support, fresh, 0.0).astype(bf16)
            state_ref[first + g, pl.ds(row, 16), :] = fresh
            states[g] = fresh.astype(f32)
        return carry

    lax.fori_loop(0, 2 * BINS, update, 0)
    for s in range(SLOTS):
        first = (s // LAYERS) * COLOURS
        own_ref[s] = state_ref[first + colour_ref[tile * SLOTS + s]]
        out_ref[s] = state_ref[first + colour_ref[beside * SLOTS + s]]


def patch_kernel(rows_ref, cols_ref, own_ref, recv_ref, sib_own_ref, sib_recv_ref, out_ref):
    core = lax.axis_index("frame")
    line = iota((PATCH, EDGE), 1)
    block = line // HALF
    home = jnp.where(core == 0, HALF, 2 * HALF)
    edge = jnp.where(core == 0, 0, 3 * HALF)
    far_home = 3 * HALF - home
    far_edge = 3 * HALF - edge
    base = jnp.where(block == 0, home, jnp.where(block == 1, edge, jnp.where(block == 2, far_home, far_edge)))
    row_at = base + line % HALF - HALF - iota((PATCH, EDGE), 0)
    col_at = iota((EDGE, PATCH), 0) - iota((EDGE, PATCH), 1)
    for s in range(SLOTS):
        row_pick = jnp.where(row_at == rows_ref[s], 1.0, 0.0).astype(bf16)
        col_pick = jnp.where(col_at == cols_ref[s], 1.0, 0.0).astype(bf16)
        whole = jnp.concatenate([own_ref[s], recv_ref[s], sib_own_ref[s], sib_recv_ref[s]], axis=0)
        lifted = dot(row_pick, whole).astype(bf16)
        out_ref[s] = dot(lifted, col_pick).astype(bf16)


def shape(dims, dtype=f32):
    return jax.ShapeDtypeStruct(dims, dtype)


def call(kernel, ins, outs, name, limit, scratch=(), out_specs=None):
    return pl.pallas_call(
        kernel,
        in_specs=ins,
        out_specs=out_specs or [vmem] * len(outs),
        out_shape=outs,
        scratch_shapes=list(scratch),
        name=name,
        compiler_params=pltpu.CompilerParams(vmem_limit_bytes=limit * 2**20),
    )


def on_device(movie_block, patches, patch_rows, patch_cols, neuron_live, neuron_colour, traces):
    tiles = lax.axis_size("tile")
    swap_pairs = []
    for t in range(tiles - 1):
        swap_pairs += [(2 * t + 1, 2 * t + 2), (2 * t + 2, 2 * t + 1)]

    def pair_swap(value):
        return lax.ppermute(value, ("tile", "frame"), swap_pairs)

    def chip_swap(value):
        return lax.ppermute(value, "frame", [(0, 1), (1, 0)])

    piece = shape((SLOTS, HALF, EDGE), bf16)
    strip = shape((64, HALF, 512), bf16)
    group = shape((GROUP, FRAMES))
    hbm = pl.BlockSpec(memory_space=pltpu.HBM)
    movie_block = pltpu.with_memory_space_constraint(movie_block, pltpu.HBM)
    piece_out, piece_own, movie_mine, movie_out = call(
        slab_kernel,
        [smem, smem, smem, vmem, hbm],
        [piece, piece, strip, strip],
        "slabs",
        12,
        [pltpu.SemaphoreType.DMA((2,))],
    )(patch_rows, patch_cols, neuron_live, patches, movie_block)
    movie_other = chip_swap(movie_out)
    movie_kept = pltpu.with_memory_space_constraint(movie_other, pltpu.HBM)
    piece_recv = pair_swap(piece_out)
    phases, live_rows, begin, phase_count = call(
        table_kernel,
        [smem, smem, vmem],
        [
            shape((GROUP, FRAMES), jnp.int32), group, shape((SLOTS, 64)), shape((1,), jnp.int32)
        ],
        "tables",
        2,
        [pltpu.SMEM((GROUP,), jnp.int32)],
        [vmem, vmem, vmem, smem],
    )(neuron_colour, neuron_live, traces)
    begin_far = chip_swap(begin)

    slab, message = call(
        functools.partial(partial_kernel, tiles),
        [smem] + [vmem] * 6,
        [shape((GROUP, HALF, EDGE), bf16), shape((2 * GROUP + COLOURS, FRAMES))],
        "partial_sums",
        20,
    )(
        neuron_colour, movie_mine, movie_other, piece_own, piece_recv, begin, begin_far
    )

    message_far = chip_swap(message)
    message_pair = pair_swap(message)
    message_far_pair = chip_swap(message_pair)
    state, change, gram, beside = call(
        first_phase_kernel,
        [vmem] * 6,
        [shape((2 * GROUP, FRAMES)), group, shape((2 * COLOURS, FRAMES)), group],
        "first_phase",
        4,
    )(phases, live_rows, message, message_pair, message_far, message_far_pair)

    def advance(carry):
        step, state, beside, change = carry
        delta = pair_swap(change)
        far_delta = chip_swap(delta)
        state, change, beside = call(
            next_phase_kernel,
            [smem] + [vmem] * 7,
            [shape((2 * GROUP, FRAMES)), group, group],
            "next_phase",
            4,
        )(step.reshape(1), phases, live_rows, gram, state, beside, delta, far_delta)
        return step + 1, state, beside, change

    carry = advance((jnp.int32(1), state, beside, change))
    _, state, beside, change = lax.while_loop(lambda c: c[0] < phase_count[0], advance, carry)
    delta = pair_swap(change)

    new_traces, final_out, final_own = call(
        functools.partial(spatial_kernel, tiles),
        [smem, vmem, hbm] + [vmem] * 4,
        [shape((SLOTS, 64)), piece, piece],
        "spatial",
        20,
        [
            pltpu.VMEM((256, 2048), bf16),
            pltpu.VMEM((GROUP * COLOURS, EDGE), f32),
            pltpu.VMEM((BINS, 256, 256), f32),
            pltpu.VMEM((GROUP, HALF, EDGE), bf16),
            pltpu.VMEM((64, HALF, 512), bf16),
            pltpu.SemaphoreType.DMA(()),
        ],
    )(neuron_colour, movie_mine, movie_kept, slab, state, beside, delta)

    far_own = chip_swap(final_own)
    final_recv = pair_swap(final_out)
    far_recv = chip_swap(final_recv)
    (new_patches,) = call(
        patch_kernel,
        [smem, smem] + [vmem] * 4,
        [shape((SLOTS, PATCH, PATCH), bf16)],
        "patches",
        8,
    )(patch_rows, patch_cols, final_own, final_recv, far_own, far_recv)
    return (new_traces, new_patches)


def solution(mesh):
    placed = (
        P("frame", "tile", None),
        P("tile", None, None),
        P("tile"),
        P("tile"),
        P("tile"),
        P(),
        P("tile", "frame"),
    )
    return jax.shard_map(
        on_device,
        mesh=mesh,
        in_specs=placed,
        out_specs=(P("tile", "frame"), P("tile", None, None)),
        check_vma=False,
    )
```

```python
import functools

import jax
import jax.numpy as jnp
from jax import lax
from jax.experimental import pallas as pl
from jax.experimental.pallas import tpu as pltpu
from jax.sharding import PartitionSpec as P

exact = lax.Precision.HIGHEST
f32 = jnp.float32
bf16 = jnp.bfloat16
BINS = 4
LAYERS = 8
SLOTS = 32
COLOURS = 16
PATCH = 64
HALF = 32
EDGE = 128
FRAMES = 128
GROUP = BINS * COLOURS
floor_share = 0.25

vmem = pl.BlockSpec(memory_space=pltpu.VMEM)
smem = pl.BlockSpec(memory_space=pltpu.SMEM)


def iota(shape, dim):
    return lax.broadcasted_iota(jnp.int32, shape, dim)


def dot_nt(a, b, precision=None):
    return lax.dot_general(
        a, b, (((1,), (1,)), ((), ())), precision=precision, preferred_element_type=f32
    )


def dot(a, b, precision=None):
    return lax.dot_general(
        a, b, (((1,), (0,)), ((), ())), precision=precision, preferred_element_type=f32
    )


def neighbour_tile(tile, core, tiles):
    other = jnp.where(core == 0, tile - 1, tile + 1)
    other = jnp.where(other < 0, tile + 1, other)
    return jnp.where(other >= tiles, tile - 1, other)


def slab_kernel(
    rows_ref, cols_ref, live_ref, patches_ref, out_ref, own_ref, raw_ref, pad_ref, sems,
):
    core = lax.axis_index("frame")
    chunk = SLOTS // 4
    fetches = []
    for i in range(4):
        part = slice(i * chunk, (i + 1) * chunk)
        fetches.append(pltpu.make_async_copy(patches_ref.at[part], raw_ref.at[part], sems.at[i]))
        fetches[i].start()
    zeros = jnp.zeros((PATCH, EDGE), f32)
    blank = jnp.zeros((PATCH, PATCH), f32)
    for s in range(SLOTS):
        pad_ref[s, :PATCH, :] = zeros
        pad_ref[s, 2 * PATCH :, :] = zeros
    for s in range(SLOTS):
        if s % chunk == 0:
            fetches[s // chunk].wait()
        filled = jnp.where(live_ref[s] > 0, raw_ref[s].astype(f32), 0.0)
        pad_ref[s, PATCH : 2 * PATCH, :] = jnp.concatenate([filled, blank], axis=1)
        start = jnp.where(core == 0, HALF, PATCH + HALF) - rows_ref[s]
        window = pad_ref[s, pl.ds(start, PATCH), :]
        window = pltpu.roll(window, cols_ref[s], 1).astype(bf16)
        upper, lower = window[:HALF], window[HALF:]
        out_ref[s] = jnp.where(core == 0, upper, lower)
        own_ref[s] = jnp.where(core == 0, lower, upper)


def fetch_kernel(live_ref, traces_ref, movie_ref, begin_ref, strip_ref, sems):
    first = pl.multiple_of(HALF * lax.axis_index("frame"), HALF)
    fetches = fetch_rows(movie_ref, strip_ref, first, sems)
    for s in range(SLOTS):
        begin_ref[s : s + 1, :] = traces_ref[s : s + 1, :] * live_ref[s].astype(f32)
    for fetch in fetches:
        fetch.wait()


def table_kernel(colour_ref, anchor_ref, phase_ref, repeat_ref, count_ref, owner_ref):
    tile = lax.axis_index("tile")
    for i in range(GROUP):
        owner_ref[i] = 0
    for s in range(SLOTS):
        at = (s // LAYERS) * COLOURS + colour_ref[tile * SLOTS + s]
        owner_ref[at] = 1
    most = jnp.int32(0)
    for b in range(BINS):
        phase = jnp.int32(0)
        for g in range(COLOURS):
            i = b * COLOURS + g
            if g:
                phase = phase + jnp.abs(owner_ref[i] - owner_ref[i - 1])
            value = phase + 100 * (1 - owner_ref[i])
            phase_ref[i : i + 1, :] = jnp.full((1, FRAMES), value, jnp.int32)
        most = jnp.maximum(most, phase + 1)
    count_ref[0] = most
    position = (iota((FRAMES, 1024), 1) // 8 + 64 * lax.axis_index("frame")) % FRAMES
    repeat_ref[...] = jnp.where(position == iota((FRAMES, 1024), 0), 1.0, 0.0).astype(bf16)


def fetch_rows(movie_ref, strip_ref, first, sems):
    fetches = []
    for i in range(8):
        part = slice(8 * i, 8 * i + 8)
        rows = movie_ref.at[part, pl.ds(first, HALF), :]
        fetches.append(pltpu.make_async_copy(rows, strip_ref.at[part], sems.at[i]))
        fetches[-1].start()
    return fetches


def strips(ref, items, first, lanes):
    parts = []
    for q in range(HALF // 8):
        part = ref[items, pl.ds(pl.multiple_of(first + 8 * q, 8), 8), lanes]
        parts.append(part.reshape(part.shape[0] * 8, EDGE))
    return jnp.concatenate(parts, axis=1)


def partial_kernel(
    tiles, colour_ref, mine_ref, other_ref, own_ref, recv_ref, near_ref, far_ref,
    slab_ref, message_ref, kept_ref, *refs
):
    pixels_refs, (laid_ref, sems) = refs[:BINS], refs[BINS:]
    tile = lax.axis_index("tile")
    core = lax.axis_index("frame")
    beside = neighbour_tile(tile, core, tiles)
    message_ref[...] = jnp.zeros_like(message_ref)
    start = GROUP + COLOURS
    wide = jnp.concatenate([near_ref[...], far_ref[...]], axis=1)
    swapped = jnp.concatenate([far_ref[...], near_ref[...]], axis=1)
    first = jnp.where(core == 0, wide, swapped)
    for s in range(SLOTS):
        b = s // LAYERS
        mine = b * COLOURS + colour_ref[tile * SLOTS + s]
        theirs = b * COLOURS + colour_ref[beside * SLOTS + s]
        slab_ref[mine] = own_ref[s]
        slab_ref[theirs] = recv_ref[s]
        message_ref[pl.ds(start + mine, 1), :] = first[s : s + 1]
    same_row = iota((512, 128), 0) % 8 == iota((512, 128), 1) % 8
    fold = jnp.where(iota((COLOURS, 384), 1) % 128 // 8 == iota((COLOURS, 384), 0), 1.0, 0.0)
    parts = {}
    grams = []
    keeps = []
    boths = []
    for i, ref in enumerate((mine_ref, other_ref)):
        for b in range(BINS):
            if i == 0:
                both = strips(slab_ref, slice(b * COLOURS, (b + 1) * COLOURS), 0, slice(0, EDGE))
                boths.append(both)
                square = jnp.where(same_row[:128], dot_nt(both, both), 0.0)
                grams.append(jnp.sum(square.reshape(COLOURS, 8, 128), axis=1))
            pixels = strips(ref, slice(0, 64), i * HALF * core, slice(b * EDGE, (b + 1) * EDGE))
            if i == 0:
                laid_ref[b] = pixels
                keeps.append(pltpu.make_async_copy(laid_ref.at[b], kept_ref.at[b], sems.at[b]))
                keeps[-1].start()
            else:
                pixels_refs[b][...] = pixels
            product = jnp.where(same_row, dot_nt(pixels, boths[b]), 0.0)
            parts[b, i] = jnp.sum(product.reshape(64, 8, 128), axis=1)
    drives = []
    for b in range(BINS):
        near = jnp.concatenate([parts[b, 0], parts[b, 1]], axis=0)
        far = jnp.concatenate([parts[b, 1], parts[b, 0]], axis=0)
        drives.append(jnp.where(core == 0, near, far))
    drive = dot_nt(fold.astype(bf16), three_parts(jnp.concatenate(drives, axis=0)))
    for b in range(BINS):
        message_ref[b * COLOURS : (b + 1) * COLOURS, :] = drive[:, b * FRAMES : (b + 1) * FRAMES]
    spread = jnp.where(iota((384, EDGE), 0) % 128 // 8 == iota((384, EDGE), 1) % 16, 1.0, 0.0)
    gram = dot(three_parts(jnp.concatenate(grams, axis=0)), spread.astype(bf16))
    lane = iota((COLOURS, EDGE), 1) // COLOURS
    total = jnp.zeros((COLOURS, EDGE), f32)
    for b in range(BINS):
        total = jnp.where(lane == b, gram[b * COLOURS : (b + 1) * COLOURS], total)
    message_ref[GROUP : GROUP + COLOURS, :] = total
    for keep in keeps:
        keep.wait()


def three_parts(value):
    high = value.astype(bf16)
    rest = value - high.astype(f32)
    middle = rest.astype(bf16)
    low = (rest - middle.astype(f32)).astype(bf16)
    return jnp.concatenate([high, middle, low], axis=1)


def block_diagonal(gram):
    tall = jnp.concatenate([gram] * BINS, axis=0)[:, :GROUP]
    keep = iota((GROUP, GROUP), 0) // COLOURS == iota((GROUP, GROUP), 1) // COLOURS
    return jnp.where(keep, tall, 0.0)


def settle(phase_ref, live_ref, gram, residual, current, phase, state_ref, change_ref):
    whole = jnp.concatenate([gram] * BINS, axis=0)
    lane = iota((GROUP, EDGE), 1)
    diag = jnp.sum(jnp.where(lane == iota((GROUP, EDGE), 0), whole, 0.0), axis=1, keepdims=True)
    inverse = 1.0 / (diag + (1.0 - live_ref[...]))
    chosen = phase_ref[...] == phase
    news = []
    changes = []
    for b in range(BINS):
        rows = slice(b * COLOURS, (b + 1) * COLOURS)
        rest, now = residual[rows], current[rows]
        inv, pick = inverse[rows], chosen[rows]
        row_id = iota((COLOURS, FRAMES), 0)
        change = jnp.zeros((COLOURS, FRAMES), f32)
        for g in range(COLOURS):
            at = slice(g, g + 1)
            value = jnp.maximum(now[at] + rest[at] * inv[at], 0.0) - now[at]
            delta = jnp.where(pick[at], value, 0.0)
            lane_at = slice(b * COLOURS + g, b * COLOURS + g + 1)
            column = jnp.broadcast_to(gram[:, lane_at], (COLOURS, FRAMES))
            rest = rest - column * delta
            change = jnp.where(row_id == g, delta, change)
        state_ref[rows, :] = rest
        state_ref[GROUP + b * COLOURS : GROUP + (b + 1) * COLOURS, :] = now + change
        change_ref[rows, :] = change


def pack_kernel(mine_ref, far_ref, out_ref):
    out_ref[:GROUP, :] = mine_ref[:GROUP, :]
    out_ref[GROUP : 2 * GROUP, :] = far_ref[:GROUP, :]
    grams = slice(GROUP, GROUP + COLOURS)
    out_ref[2 * GROUP : 2 * GROUP + COLOURS, :] = mine_ref[grams, :]
    out_ref[2 * GROUP + COLOURS : 2 * GROUP + 2 * COLOURS, :] = far_ref[grams, :]
    out_ref[2 * GROUP + 2 * COLOURS :, :] = mine_ref[GROUP + COLOURS :, :]


near_drive = slice(0, GROUP)
far_drive = slice(GROUP, 2 * GROUP)
near_gram = slice(2 * GROUP, 2 * GROUP + COLOURS)
far_gram = slice(2 * GROUP + COLOURS, 2 * GROUP + 2 * COLOURS)
all_traces = slice(2 * GROUP + 2 * COLOURS, 3 * GROUP + 2 * COLOURS)
PACKED = 3 * GROUP + 2 * COLOURS


def forward_kernel(tiles, pack_ref, pair_ref, anchor_ref, out_ref):
    tile = lax.axis_index("tile")
    core = lax.axis_index("frame")
    last = ((tile == 0) & (core == 0)) | ((tile == tiles - 1) & (core == 1))
    alone = jnp.where(last, 1.0, 0.0)
    out_ref[near_drive, :] = pack_ref[near_drive, :] + pair_ref[near_drive, :]
    out_ref[far_drive, :] = pair_ref[far_drive, :] + alone * pack_ref[far_drive, :]
    out_ref[near_gram, :] = pack_ref[near_gram, :] + pair_ref[near_gram, :]
    out_ref[far_gram, :] = pair_ref[far_gram, :] + alone * pack_ref[far_gram, :]
    out_ref[all_traces, :] = pack_ref[all_traces, :] + pair_ref[all_traces, :]


side_drives = [slice(i * GROUP, (i + 1) * GROUP) for i in range(3)]
side_grams = [slice(3 * GROUP + i * COLOURS, 3 * GROUP + (i + 1) * COLOURS) for i in range(3)]
side_next = slice(3 * GROUP + 3 * COLOURS, 4 * GROUP + 3 * COLOURS)
side_beyond = slice(4 * GROUP + 3 * COLOURS, 5 * GROUP + 3 * COLOURS)
SIDE = 5 * GROUP + 3 * COLOURS


def side_kernel(pack_ref, pair_ref, beyond_ref, out_ref):
    out_ref[side_drives[0], :] = pack_ref[near_drive, :] + pair_ref[near_drive, :]
    out_ref[side_drives[1], :] = pair_ref[far_drive, :] + beyond_ref[far_drive, :]
    out_ref[side_drives[2], :] = beyond_ref[near_drive, :]
    out_ref[side_grams[0], :] = pack_ref[near_gram, :] + pair_ref[near_gram, :]
    out_ref[side_grams[1], :] = pair_ref[far_gram, :] + beyond_ref[far_gram, :]
    out_ref[side_grams[2], :] = beyond_ref[near_gram, :]
    out_ref[side_next, :] = pair_ref[all_traces, :]
    out_ref[side_beyond, :] = beyond_ref[all_traces, :]


def settler(gram):
    whole = jnp.concatenate([gram] * BINS, axis=0)
    diag = jnp.where(iota((GROUP, EDGE), 1) == iota((GROUP, EDGE), 0), whole, 0.0)
    diag = jnp.sum(diag, axis=1, keepdims=True)
    inverse = jnp.broadcast_to(1.0 / jnp.where(diag > 0.0, diag, 1.0), (GROUP, FRAMES))
    row_id = iota((COLOURS, FRAMES), 0)

    def settle(residual, current, chosen):
        rests, changes = [], []
        for b in range(BINS):
            rows = slice(b * COLOURS, (b + 1) * COLOURS)
            rest, now, inv, pick = residual[rows], current[rows], inverse[rows], chosen[rows]
            change = jnp.zeros((COLOURS, FRAMES), f32)
            for g in range(COLOURS):
                at = slice(g, g + 1)
                value = jnp.maximum(now[at] + rest[at] * inv[at], 0.0) - now[at]
                delta = jnp.where(pick[at], value, 0.0)
                lane_at = slice(b * COLOURS + g, b * COLOURS + g + 1)
                rest = rest - jnp.broadcast_to(gram[:, lane_at], (COLOURS, FRAMES)) * delta
                change = jnp.where(row_id == g, delta, change)
            rests.append(rest)
            changes.append(change)
        return jnp.concatenate(rests, axis=0), jnp.concatenate(changes, axis=0)

    return settle


def window_kernel(
    phase_ref, pack_ref, here_ref, there_ref, state_ref, change_ref, gram_ref, before_ref, beside_ref
):
    phase = phase_ref[...]
    own = phase < 100
    start = pack_ref[all_traces, :]
    sides = []
    for ref in (here_ref, there_ref):
        grams = [ref[at, :] for at in side_grams]
        near, beyond = ref[side_next, :], ref[side_beyond, :]
        second = jnp.where(own, beyond, 0.0)
        blocks = [block_diagonal(gram) for gram in grams]
        held = [start + near, near + second, beyond]
        parts = [ref[side_drives[i], :] - dot(blocks[i], held[i], exact) for i in range(3)]
        sides.append((grams, blocks, parts, near, second))
    (grams_a, blocks_a, parts_a, near_a, second_a), (grams_b, blocks_b, parts_b, near_b, second_b) = sides
    mine_now, theirs_now = phase == 0, phase == 100
    settle_own = settler(grams_a[0] + grams_b[0])
    settle_near = settler(grams_a[0] + grams_a[1])
    rest, change = settle_own(parts_a[0] + parts_b[0], start, mine_now)
    rest_a, near_change_a = settle_near(parts_a[0] + parts_a[1], near_a, theirs_now)
    _, near_change_b = settler(grams_b[0] + grams_b[1])(parts_b[0] + parts_b[1], near_b, theirs_now)
    _, second_change = settler(grams_a[1] + grams_a[2])(parts_a[1] + parts_a[2], second_a, mine_now)
    rest = rest - dot(blocks_a[0], near_change_a, exact) - dot(blocks_b[0], near_change_b, exact)
    rest_a = rest_a - dot(blocks_a[0], change, exact) - dot(blocks_a[1], second_change, exact)
    now = start + change
    near_now = near_a + near_change_a
    rest, late = settle_own(rest, now, phase == 1)
    _, near_late = settle_near(rest_a, near_now, phase == 101)
    state_ref[:GROUP, :] = rest
    state_ref[GROUP:, :] = now + late
    change_ref[...] = late
    gram_ref[:COLOURS, :] = grams_a[0]
    gram_ref[COLOURS:, :] = grams_b[0]
    before_ref[...] = near_now
    beside_ref[...] = near_now + near_late


def next_phase_kernel(
    step_ref, phase_ref, gram_ref, old_ref, before_ref, delta_ref, far_delta_ref,
    state_ref, change_ref, before_out_ref,
):
    here = gram_ref[:COLOURS, :]
    there = gram_ref[COLOURS:, :]
    coupled = dot(block_diagonal(here), delta_ref[...], exact)
    coupled = coupled + dot(block_diagonal(there), far_delta_ref[...], exact)
    now = old_ref[GROUP:, :]
    chosen = phase_ref[...] == step_ref[0]
    rest, change = settler(here + there)(old_ref[:GROUP, :] - coupled, now, chosen)
    state_ref[:GROUP, :] = rest
    state_ref[GROUP:, :] = now + change
    change_ref[...] = change
    before_out_ref[...] = before_ref[...] + delta_ref[...]


def spatial_kernel(
    tiles, colour_ref, repeat_ref, *refs
):
    far_refs, refs = refs[:BINS], refs[BINS:]
    kept_ref, slab_ref, state_in_ref, beside_ref, out_ref, own_ref = refs[:6]
    weight_ref, cross_ref, field_ref, state_ref, near_ref, sems = refs[6:]
    fetches = []
    for b in range(BINS):
        fetches.append(pltpu.make_async_copy(kept_ref.at[b], near_ref.at[b], sems.at[b]))
        fetches[-1].start()
    tile = lax.axis_index("tile")
    core = lax.axis_index("frame")
    beside = neighbour_tile(tile, core, tiles)
    both = state_in_ref[GROUP:, :] + beside_ref[...]
    repeated = dot(both.astype(bf16), repeat_ref[...])
    same_row = iota((8, 1024), 0) == iota((8, 1024), 1) % 8
    for b in range(BINS):
        for g in range(0, COLOURS, 2):
            pair = []
            for i in range(2):
                line = repeated[b * COLOURS + g + i : b * COLOURS + g + i + 1]
                pair.append(jnp.where(same_row, line, 0.0))
            weight_ref[b, 8 * g : 8 * g + 16, :] = jnp.concatenate(pair, axis=0).astype(bf16)
        field_ref[b] = dot(weight_ref[b, :, 512:], far_refs[b][...])
    for b in range(BINS):
        rows = slice(b * COLOURS, (b + 1) * COLOURS)
        now = both[rows]
        cross = dot_nt(now, now, exact)
        for g in range(COLOURS):
            column = jnp.broadcast_to(cross[:, g : g + 1], (COLOURS, EDGE))
            cross_ref[(b * COLOURS + g) * 16 : (b * COLOURS + g) * 16 + 16, :] = column
    for b in range(BINS):
        fetches[b].wait()
        field_ref[b] = field_ref[b] + dot(weight_ref[b, :, :512], near_ref[b])

    floor = floor_share * FRAMES

    def update(step, carry):
        b = step // 2
        q = step % 2
        first = b * COLOURS
        row = pl.multiple_of(q * 16, 16)
        states = [
            slab_ref[first + m, pl.ds(row, 16), :].astype(f32) for m in range(COLOURS)
        ]
        for g in range(COLOURS):
            base = (first + g) * 16
            support = states[g] > 0.0
            field = jnp.concatenate(
                [
                    field_ref[b, 8 * g : 8 * g + 8, pl.ds(pl.multiple_of((2 * q + i) * EDGE, EDGE), EDGE)]
                    for i in range(2)
                ],
                axis=0,
            )
            rest = field
            for m in list(range(g, COLOURS)) + list(range(g)):
                rest = rest - cross_ref[pl.ds(base + m, 1), :] * states[m]
            scale = 1.0 / jnp.maximum(cross_ref[pl.ds(base + g, 1), :], floor)
            fresh = jnp.maximum(states[g] + rest * scale, 0.0)
            fresh = jnp.where(support, fresh, 0.0).astype(bf16)
            state_ref[first + g, pl.ds(row, 16), :] = fresh
            states[g] = fresh.astype(f32)
        return carry

    lax.fori_loop(0, 2 * BINS, update, 0)
    for s in range(SLOTS):
        first = (s // LAYERS) * COLOURS
        own_ref[s] = state_ref[first + colour_ref[tile * SLOTS + s]]
        out_ref[s] = state_ref[first + colour_ref[beside * SLOTS + s]]


def patch_kernel(
    rows_ref, cols_ref, colour_ref, state_ref, own_ref, recv_ref, sib_own_ref, sib_recv_ref,
    out_ref, traces_ref, framed_ref,
):
    tile = lax.axis_index("tile")
    own = state_ref[GROUP:, :]
    rolled = jnp.concatenate([own[:, 64:], own[:, :64]], axis=1)
    framed_ref[...] = jnp.where(lax.axis_index("frame") == 0, own, rolled)[:, :64]
    core = lax.axis_index("frame")
    line = iota((PATCH, EDGE), 1)
    block = line // HALF
    home = jnp.where(core == 0, HALF, 2 * HALF)
    edge = jnp.where(core == 0, 0, 3 * HALF)
    far_home = 3 * HALF - home
    far_edge = 3 * HALF - edge
    base = jnp.where(block == 0, home, jnp.where(block == 1, edge, jnp.where(block == 2, far_home, far_edge)))
    row_at = base + line % HALF - HALF - iota((PATCH, EDGE), 0)
    col_at = iota((EDGE, PATCH), 0) - iota((EDGE, PATCH), 1)
    for s in range(SLOTS):
        at = (s // LAYERS) * COLOURS + colour_ref[tile * SLOTS + s]
        traces_ref[s : s + 1, :] = framed_ref[pl.ds(at, 1), :]
        row_pick = jnp.where(row_at == rows_ref[s], 1.0, 0.0).astype(bf16)
        col_pick = jnp.where(col_at == cols_ref[s], 1.0, 0.0).astype(bf16)
        whole = jnp.concatenate([own_ref[s], recv_ref[s], sib_own_ref[s], sib_recv_ref[s]], axis=0)
        lifted = dot(row_pick, whole).astype(bf16)
        out_ref[s] = dot(lifted, col_pick).astype(bf16)


def shape(dims, dtype=f32):
    return jax.ShapeDtypeStruct(dims, dtype)


def call(kernel, ins, outs, name, limit, scratch=(), out_specs=None):
    return pl.pallas_call(
        kernel,
        in_specs=ins,
        out_specs=out_specs or [vmem] * len(outs),
        out_shape=outs,
        scratch_shapes=list(scratch),
        name=name,
        compiler_params=pltpu.CompilerParams(vmem_limit_bytes=limit * 2**20),
    )


def on_device(movie_block, patches, patch_rows, patch_cols, neuron_live, neuron_colour, traces):
    tiles = lax.axis_size("tile")
    swap_pairs = []
    for t in range(tiles - 1):
        swap_pairs += [(2 * t + 1, 2 * t + 2), (2 * t + 2, 2 * t + 1)]

    def pair_swap(value):
        return lax.ppermute(value, ("tile", "frame"), swap_pairs)

    far_pairs = [(2 * (tiles - 1) + 1, 2 * (tiles - 3) + 1), (0, 4)]
    for t in range(tiles - 3):
        far_pairs += [(2 * t + 1, 2 * (t + 3)), (2 * (t + 3), 2 * t + 1)]

    def chip_swap(value):
        return lax.ppermute(value, "frame", [(0, 1), (1, 0)])

    def in_hbm(value):
        return pltpu.with_memory_space_constraint(value, pltpu.HBM)

    piece = shape((SLOTS, HALF, EDGE), bf16)
    group = shape((GROUP, FRAMES))
    hbm = pl.BlockSpec(memory_space=pltpu.HBM)
    movie_far = chip_swap(movie_block)
    piece_out, piece_own = call(
        slab_kernel,
        [smem, smem, smem, hbm],
        [piece, piece],
        "slabs",
        8,
        [
            pltpu.VMEM((SLOTS, PATCH, PATCH), bf16),
            pltpu.VMEM((SLOTS, 3 * PATCH, EDGE), f32),
            pltpu.SemaphoreType.DMA((4,)),
        ],
    )(in_hbm(patch_rows), in_hbm(patch_cols), in_hbm(neuron_live), in_hbm(patches))
    piece_recv = pair_swap(piece_out)
    begin, movie_strip = call(
        fetch_kernel,
        [smem, vmem, hbm],
        [shape((SLOTS, 64)), shape((64, HALF, 512), bf16)],
        "fetch",
        4,
        [pltpu.SemaphoreType.DMA((8,))],
    )(in_hbm(neuron_live), in_hbm(traces), in_hbm(movie_block))
    begin_far = chip_swap(begin)

    slab, message, kept, *far_pixels = call(
        functools.partial(partial_kernel, tiles),
        [smem] + [vmem] * 6,
        [
            shape((GROUP, HALF, EDGE), bf16), shape((2 * GROUP + COLOURS, FRAMES)),
            pltpu.HBM((BINS, 512, 512), bf16),
        ]
        + [shape((512, 512), bf16)] * BINS,
        "partial_sums",
        12,
        [pltpu.VMEM((BINS, 512, 512), bf16), pltpu.SemaphoreType.DMA((BINS,))],
        [vmem, vmem, hbm] + [vmem] * BINS,
    )(neuron_colour, movie_strip, movie_far, piece_own, piece_recv, begin, begin_far)

    packed_shape, side_shape = shape((PACKED, FRAMES)), shape((SIDE, FRAMES))
    state_shape = shape((2 * GROUP, FRAMES))
    (packed,) = call(pack_kernel, [vmem] * 2, [packed_shape], "pack", 2)(message, chip_swap(message))
    pair = pair_swap(packed)
    phases, repeat, phase_count = call(
        table_kernel,
        [smem, vmem],
        [shape((GROUP, FRAMES), jnp.int32), shape((FRAMES, 1024), bf16), shape((1,), jnp.int32)],
        "tables",
        2,
        [pltpu.SMEM((GROUP,), jnp.int32)],
        [vmem, vmem, smem],
    )(neuron_colour, packed)
    (onward,) = call(
        functools.partial(forward_kernel, tiles), [vmem] * 3, [packed_shape], "forward", 2
    )(packed, pair, phases)
    beyond = lax.ppermute(onward, ("tile", "frame"), far_pairs)
    (side,) = call(side_kernel, [vmem] * 3, [side_shape], "side", 2)(packed, pair, beyond)
    state, change, gram, before, beside = call(
        window_kernel,
        [vmem] * 4,
        [state_shape, group, shape((2 * COLOURS, FRAMES)), group, group],
        "window",
        8,
    )(phases, packed, side, chip_swap(side))

    def advance(carry):
        step, state, before, change, _ = carry
        delta = pair_swap(change)
        state, change, before = call(
            next_phase_kernel, [smem] + [vmem] * 6, [state_shape, group, group], "next_phase", 4
        )(step.reshape(1), phases, gram, state, before, delta, chip_swap(delta))
        return step + 1, state, before, change, before + pair_swap(change)

    carry = (jnp.int32(2), state, before, change, beside)
    _, state, _, _, beside = lax.while_loop(lambda c: c[0] < phase_count[0], advance, carry)

    final_out, final_own = call(
        functools.partial(spatial_kernel, tiles),
        [smem] + [vmem] * 5 + [hbm] + [vmem] * 3,
        [piece, piece],
        "spatial",
        10,
        [
            pltpu.VMEM((BINS, 128, 1024), bf16),
            pltpu.VMEM((GROUP * COLOURS, EDGE), f32),
            pltpu.VMEM((BINS, 128, 512), f32),
            pltpu.VMEM((GROUP, HALF, EDGE), bf16),
            pltpu.VMEM((BINS, 512, 512), bf16),
            pltpu.SemaphoreType.DMA((BINS,)),
        ],
    )(neuron_colour, repeat, *far_pixels, in_hbm(kept), slab, state, beside)

    far_own = chip_swap(final_own)
    final_recv = pair_swap(final_out)
    far_recv = chip_swap(final_recv)
    new_patches, new_traces = call(
        patch_kernel,
        [smem] * 3 + [vmem] * 5,
        [shape((SLOTS, PATCH, PATCH), bf16), shape((SLOTS, 64))],
        "patches",
        8,
        [pltpu.VMEM((GROUP, 64), f32)],
    )(patch_rows, patch_cols, neuron_colour, state, final_own, final_recv, far_own, far_recv)
    return (new_traces, new_patches)


def solution(mesh):
    placed = (
        P("frame", "tile", None),
        P("tile", None, None),
        P("tile"),
        P("tile"),
        P("tile"),
        P(),
        P("tile", "frame"),
    )
    return jax.shard_map(
        on_device,
        mesh=mesh,
        in_specs=placed,
        out_specs=(P("tile", "frame"), P("tile", None, None)),
        check_vma=False,
    )
```

```python
import functools

import jax
import jax.numpy as jnp
from jax import lax
from jax.experimental import pallas as pl
from jax.experimental.pallas import tpu as pltpu
from jax.sharding import PartitionSpec as P

exact = lax.Precision.HIGHEST
f32 = jnp.float32
bf16 = jnp.bfloat16
BINS = 4
LAYERS = 8
SLOTS = 32
COLOURS = 16
PATCH = 64
HALF = 32
EDGE = 128
FRAMES = 128
GROUP = BINS * COLOURS
floor_share = 0.25

vmem = pl.BlockSpec(memory_space=pltpu.VMEM)
smem = pl.BlockSpec(memory_space=pltpu.SMEM)


def iota(shape, dim):
    return lax.broadcasted_iota(jnp.int32, shape, dim)


def dot_nt(a, b, precision=None):
    return lax.dot_general(
        a, b, (((1,), (1,)), ((), ())), precision=precision, preferred_element_type=f32
    )


def dot(a, b, precision=None):
    return lax.dot_general(
        a, b, (((1,), (0,)), ((), ())), precision=precision, preferred_element_type=f32
    )


def neighbour_tile(tile, core, tiles):
    other = jnp.where(core == 0, tile - 1, tile + 1)
    other = jnp.where(other < 0, tile + 1, other)
    return jnp.where(other >= tiles, tile - 1, other)


def slab_kernel(
    rows_ref, cols_ref, live_ref, patches_ref, out_ref, own_ref, raw_ref, pad_ref, sems,
):
    core = lax.axis_index("frame")
    chunk = SLOTS // 4
    fetches = []
    for i in range(4):
        part = slice(i * chunk, (i + 1) * chunk)
        fetches.append(pltpu.make_async_copy(patches_ref.at[part], raw_ref.at[part], sems.at[i]))
        fetches[i].start()
    zeros = jnp.zeros((PATCH, EDGE), f32)
    blank = jnp.zeros((PATCH, PATCH), f32)
    for s in range(SLOTS):
        pad_ref[s, :PATCH, :] = zeros
        pad_ref[s, 2 * PATCH :, :] = zeros
    for s in range(SLOTS):
        if s % chunk == 0:
            fetches[s // chunk].wait()
        filled = jnp.where(live_ref[s] > 0, raw_ref[s].astype(f32), 0.0)
        pad_ref[s, PATCH : 2 * PATCH, :] = jnp.concatenate([filled, blank], axis=1)
        start = jnp.where(core == 0, HALF, PATCH + HALF) - rows_ref[s]
        window = pad_ref[s, pl.ds(start, PATCH), :]
        window = pltpu.roll(window, cols_ref[s], 1).astype(bf16)
        upper, lower = window[:HALF], window[HALF:]
        out_ref[s] = jnp.where(core == 0, upper, lower)
        own_ref[s] = jnp.where(core == 0, lower, upper)


def fetch_kernel(live_ref, traces_ref, movie_ref, begin_ref, strip_ref, sems):
    first = pl.multiple_of(HALF * lax.axis_index("frame"), HALF)
    fetches = fetch_rows(movie_ref, strip_ref, first, sems)
    for s in range(SLOTS):
        begin_ref[s : s + 1, :] = traces_ref[s : s + 1, :] * live_ref[s].astype(f32)
    for fetch in fetches:
        fetch.wait()


def table_kernel(colour_ref, anchor_ref, phase_ref, repeat_ref, count_ref, owner_ref):
    tile = lax.axis_index("tile")
    for i in range(GROUP):
        owner_ref[i] = 0
    for s in range(SLOTS):
        at = (s // LAYERS) * COLOURS + colour_ref[tile * SLOTS + s]
        owner_ref[at] = 1
    most = jnp.int32(0)
    for b in range(BINS):
        phase = jnp.int32(0)
        for g in range(COLOURS):
            i = b * COLOURS + g
            if g:
                phase = phase + jnp.abs(owner_ref[i] - owner_ref[i - 1])
            value = phase + 100 * (1 - owner_ref[i])
            phase_ref[i : i + 1, :] = jnp.full((1, FRAMES), value, jnp.int32)
        most = jnp.maximum(most, phase + 1)
    count_ref[...] = jnp.full((1, 1), most, jnp.int32)
    position = (iota((FRAMES, 1024), 1) // 8 + 64 * lax.axis_index("frame")) % FRAMES
    repeat_ref[...] = jnp.where(position == iota((FRAMES, 1024), 0), 1.0, 0.0).astype(bf16)


def fetch_rows(movie_ref, strip_ref, first, sems):
    fetches = []
    for i in range(8):
        part = slice(8 * i, 8 * i + 8)
        rows = movie_ref.at[part, pl.ds(first, HALF), :]
        fetches.append(pltpu.make_async_copy(rows, strip_ref.at[part], sems.at[i]))
        fetches[-1].start()
    return fetches


def strips(ref, items, first, lanes):
    parts = []
    for q in range(HALF // 8):
        part = ref[items, pl.ds(pl.multiple_of(first + 8 * q, 8), 8), lanes]
        parts.append(part.reshape(part.shape[0] * 8, EDGE))
    return jnp.concatenate(parts, axis=1)


def partial_kernel(
    tiles, colour_ref, mine_ref, other_ref, own_ref, recv_ref, near_ref, far_ref,
    slab_ref, message_ref, *pixels_refs,
):
    tile = lax.axis_index("tile")
    core = lax.axis_index("frame")
    beside = neighbour_tile(tile, core, tiles)
    message_ref[...] = jnp.zeros_like(message_ref)
    start = GROUP + COLOURS
    wide = jnp.concatenate([near_ref[...], far_ref[...]], axis=1)
    swapped = jnp.concatenate([far_ref[...], near_ref[...]], axis=1)
    first = jnp.where(core == 0, wide, swapped)
    for s in range(SLOTS):
        b = s // LAYERS
        mine = b * COLOURS + colour_ref[tile * SLOTS + s]
        theirs = b * COLOURS + colour_ref[beside * SLOTS + s]
        slab_ref[mine] = own_ref[s]
        slab_ref[theirs] = recv_ref[s]
        message_ref[pl.ds(start + mine, 1), :] = first[s : s + 1]
    same_row = iota((512, 128), 0) % 8 == iota((512, 128), 1) % 8
    fold = jnp.where(iota((COLOURS, 384), 1) % 128 // 8 == iota((COLOURS, 384), 0), 1.0, 0.0)
    parts = {}
    grams = []
    boths = []
    for i, ref in enumerate((mine_ref, other_ref)):
        for b in range(BINS):
            if i == 0:
                both = strips(slab_ref, slice(b * COLOURS, (b + 1) * COLOURS), 0, slice(0, EDGE))
                boths.append(both)
                square = jnp.where(same_row[:128], dot_nt(both, both), 0.0)
                grams.append(jnp.sum(square.reshape(COLOURS, 8, 128), axis=1))
            pixels = strips(ref, slice(0, 64), i * HALF * core, slice(b * EDGE, (b + 1) * EDGE))
            pixels_refs[b][512 * i : 512 * i + 512, :] = pixels
            product = jnp.where(same_row, dot_nt(pixels, boths[b]), 0.0)
            parts[b, i] = jnp.sum(product.reshape(64, 8, 128), axis=1)
    drives = []
    for b in range(BINS):
        near = jnp.concatenate([parts[b, 0], parts[b, 1]], axis=0)
        far = jnp.concatenate([parts[b, 1], parts[b, 0]], axis=0)
        drives.append(jnp.where(core == 0, near, far))
    drive = dot_nt(fold.astype(bf16), three_parts(jnp.concatenate(drives, axis=0)))
    for b in range(BINS):
        message_ref[b * COLOURS : (b + 1) * COLOURS, :] = drive[:, b * FRAMES : (b + 1) * FRAMES]
    spread = jnp.where(iota((384, EDGE), 0) % 128 // 8 == iota((384, EDGE), 1) % 16, 1.0, 0.0)
    gram = dot(three_parts(jnp.concatenate(grams, axis=0)), spread.astype(bf16))
    lane = iota((COLOURS, EDGE), 1) // COLOURS
    total = jnp.zeros((COLOURS, EDGE), f32)
    for b in range(BINS):
        total = jnp.where(lane == b, gram[b * COLOURS : (b + 1) * COLOURS], total)
    message_ref[GROUP : GROUP + COLOURS, :] = total


def three_parts(value):
    high = value.astype(bf16)
    rest = value - high.astype(f32)
    middle = rest.astype(bf16)
    low = (rest - middle.astype(f32)).astype(bf16)
    return jnp.concatenate([high, middle, low], axis=1)


def block_diagonal(gram):
    tall = jnp.concatenate([gram] * BINS, axis=0)[:, :GROUP]
    keep = iota((GROUP, GROUP), 0) // COLOURS == iota((GROUP, GROUP), 1) // COLOURS
    return jnp.where(keep, tall, 0.0)


def settle(phase_ref, live_ref, gram, residual, current, phase, state_ref, change_ref):
    whole = jnp.concatenate([gram] * BINS, axis=0)
    lane = iota((GROUP, EDGE), 1)
    diag = jnp.sum(jnp.where(lane == iota((GROUP, EDGE), 0), whole, 0.0), axis=1, keepdims=True)
    inverse = 1.0 / (diag + (1.0 - live_ref[...]))
    chosen = phase_ref[...] == phase
    news = []
    changes = []
    for b in range(BINS):
        rows = slice(b * COLOURS, (b + 1) * COLOURS)
        rest, now = residual[rows], current[rows]
        inv, pick = inverse[rows], chosen[rows]
        row_id = iota((COLOURS, FRAMES), 0)
        change = jnp.zeros((COLOURS, FRAMES), f32)
        for g in range(COLOURS):
            at = slice(g, g + 1)
            value = jnp.maximum(now[at] + rest[at] * inv[at], 0.0) - now[at]
            delta = jnp.where(pick[at], value, 0.0)
            lane_at = slice(b * COLOURS + g, b * COLOURS + g + 1)
            column = jnp.broadcast_to(gram[:, lane_at], (COLOURS, FRAMES))
            rest = rest - column * delta
            change = jnp.where(row_id == g, delta, change)
        state_ref[rows, :] = rest
        state_ref[GROUP + b * COLOURS : GROUP + (b + 1) * COLOURS, :] = now + change
        change_ref[rows, :] = change


def pack_kernel(mine_ref, far_ref, out_ref):
    out_ref[:GROUP, :] = mine_ref[:GROUP, :]
    out_ref[GROUP : 2 * GROUP, :] = far_ref[:GROUP, :]
    grams = slice(GROUP, GROUP + COLOURS)
    out_ref[2 * GROUP : 2 * GROUP + COLOURS, :] = mine_ref[grams, :]
    out_ref[2 * GROUP + COLOURS : 2 * GROUP + 2 * COLOURS, :] = far_ref[grams, :]
    out_ref[2 * GROUP + 2 * COLOURS :, :] = mine_ref[GROUP + COLOURS :, :]


near_drive = slice(0, GROUP)
far_drive = slice(GROUP, 2 * GROUP)
near_gram = slice(2 * GROUP, 2 * GROUP + COLOURS)
far_gram = slice(2 * GROUP + COLOURS, 2 * GROUP + 2 * COLOURS)
all_traces = slice(2 * GROUP + 2 * COLOURS, 3 * GROUP + 2 * COLOURS)
PACKED = 3 * GROUP + 2 * COLOURS


def forward_kernel(tiles, pack_ref, pair_ref, anchor_ref, out_ref):
    tile = lax.axis_index("tile")
    core = lax.axis_index("frame")
    last = ((tile == 0) & (core == 0)) | ((tile == tiles - 1) & (core == 1))
    alone = jnp.where(last, 1.0, 0.0)
    out_ref[near_drive, :] = pack_ref[near_drive, :] + pair_ref[near_drive, :]
    out_ref[far_drive, :] = pair_ref[far_drive, :] + alone * pack_ref[far_drive, :]
    out_ref[near_gram, :] = pack_ref[near_gram, :] + pair_ref[near_gram, :]
    out_ref[far_gram, :] = pair_ref[far_gram, :] + alone * pack_ref[far_gram, :]
    out_ref[all_traces, :] = pack_ref[all_traces, :] + pair_ref[all_traces, :]


side_drives = [slice(i * GROUP, (i + 1) * GROUP) for i in range(3)]
side_grams = [slice(3 * GROUP + i * COLOURS, 3 * GROUP + (i + 1) * COLOURS) for i in range(3)]
side_next = slice(3 * GROUP + 3 * COLOURS, 4 * GROUP + 3 * COLOURS)
side_beyond = slice(4 * GROUP + 3 * COLOURS, 5 * GROUP + 3 * COLOURS)
SIDE = 5 * GROUP + 3 * COLOURS


def side_kernel(pack_ref, pair_ref, beyond_ref, out_ref):
    out_ref[side_drives[0], :] = pack_ref[near_drive, :] + pair_ref[near_drive, :]
    out_ref[side_drives[1], :] = pair_ref[far_drive, :] + beyond_ref[far_drive, :]
    out_ref[side_drives[2], :] = beyond_ref[near_drive, :]
    out_ref[side_grams[0], :] = pack_ref[near_gram, :] + pair_ref[near_gram, :]
    out_ref[side_grams[1], :] = pair_ref[far_gram, :] + beyond_ref[far_gram, :]
    out_ref[side_grams[2], :] = beyond_ref[near_gram, :]
    out_ref[side_next, :] = pair_ref[all_traces, :]
    out_ref[side_beyond, :] = beyond_ref[all_traces, :]


def settler(gram):
    whole = jnp.concatenate([gram] * BINS, axis=0)
    diag = jnp.where(iota((GROUP, EDGE), 1) == iota((GROUP, EDGE), 0), whole, 0.0)
    diag = jnp.sum(diag, axis=1, keepdims=True)
    inverse = jnp.broadcast_to(1.0 / jnp.where(diag > 0.0, diag, 1.0), (GROUP, FRAMES))
    row_id = iota((COLOURS, FRAMES), 0)

    def settle(residual, current, chosen):
        rests, changes = [], []
        for b in range(BINS):
            rows = slice(b * COLOURS, (b + 1) * COLOURS)
            rest, now, inv, pick = residual[rows], current[rows], inverse[rows], chosen[rows]
            change = jnp.zeros((COLOURS, FRAMES), f32)
            for g in range(COLOURS):
                at = slice(g, g + 1)
                value = jnp.maximum(now[at] + rest[at] * inv[at], 0.0) - now[at]
                delta = jnp.where(pick[at], value, 0.0)
                lane_at = slice(b * COLOURS + g, b * COLOURS + g + 1)
                rest = rest - jnp.broadcast_to(gram[:, lane_at], (COLOURS, FRAMES)) * delta
                change = jnp.where(row_id == g, delta, change)
            rests.append(rest)
            changes.append(change)
        return jnp.concatenate(rests, axis=0), jnp.concatenate(changes, axis=0)

    return settle


def window_kernel(
    count_ref, phase_ref, pack_ref, here_ref, there_ref, state_ref, change_ref, gram_ref, before_ref,
    beside_ref, left_ref,
):
    left_ref[...] = count_ref[...] - 2
    phase = phase_ref[...]
    own = phase < 100
    start = pack_ref[all_traces, :]
    sides = []
    for ref in (here_ref, there_ref):
        grams = [ref[at, :] for at in side_grams]
        near, beyond = ref[side_next, :], ref[side_beyond, :]
        second = jnp.where(own, beyond, 0.0)
        blocks = [block_diagonal(gram) for gram in grams]
        held = [start + near, near + second, beyond]
        parts = [ref[side_drives[i], :] - dot(blocks[i], held[i], exact) for i in range(3)]
        sides.append((grams, blocks, parts, near, second))
    (grams_a, blocks_a, parts_a, near_a, second_a), (grams_b, blocks_b, parts_b, near_b, second_b) = sides
    mine_now, theirs_now = phase == 0, phase == 100
    settle_own = settler(grams_a[0] + grams_b[0])
    settle_near = settler(grams_a[0] + grams_a[1])
    rest, change = settle_own(parts_a[0] + parts_b[0], start, mine_now)
    rest_a, near_change_a = settle_near(parts_a[0] + parts_a[1], near_a, theirs_now)
    _, near_change_b = settler(grams_b[0] + grams_b[1])(parts_b[0] + parts_b[1], near_b, theirs_now)
    _, second_change = settler(grams_a[1] + grams_a[2])(parts_a[1] + parts_a[2], second_a, mine_now)
    rest = rest - dot(blocks_a[0], near_change_a, exact) - dot(blocks_b[0], near_change_b, exact)
    rest_a = rest_a - dot(blocks_a[0], change, exact) - dot(blocks_a[1], second_change, exact)
    now = start + change
    near_now = near_a + near_change_a
    rest, late = settle_own(rest, now, phase == 1)
    _, near_late = settle_near(rest_a, near_now, phase == 101)
    state_ref[:GROUP, :] = rest
    state_ref[GROUP:, :] = now + late
    change_ref[...] = late
    gram_ref[:COLOURS, :] = grams_a[0]
    gram_ref[COLOURS:, :] = grams_b[0]
    before_ref[...] = near_now
    beside_ref[...] = near_now + near_late


def add_kernel(a_ref, b_ref, out_ref):
    out_ref[...] = a_ref[...] + b_ref[...]


def next_phase_kernel(
    left_ref, count_ref, phase_ref, gram_ref, old_ref, before_ref, delta_ref, far_delta_ref,
    state_ref, change_ref, before_out_ref, left_out_ref,
):
    step = count_ref[...] - left_ref[...]
    left_out_ref[...] = left_ref[...] - 1
    here = gram_ref[:COLOURS, :]
    there = gram_ref[COLOURS:, :]
    coupled = dot(block_diagonal(here), delta_ref[...], exact)
    coupled = coupled + dot(block_diagonal(there), far_delta_ref[...], exact)
    now = old_ref[GROUP:, :]
    chosen = phase_ref[...] == step
    rest, change = settler(here + there)(old_ref[:GROUP, :] - coupled, now, chosen)
    state_ref[:GROUP, :] = rest
    state_ref[GROUP:, :] = now + change
    change_ref[...] = change
    before_out_ref[...] = before_ref[...] + delta_ref[...]


def spatial_kernel(
    tiles, colour_ref, repeat_ref, *refs
):
    pixels_refs, refs = refs[:BINS], refs[BINS:]
    slab_ref, state_in_ref, beside_ref, out_ref, own_ref = refs[:5]
    weight_ref, cross_ref, field_ref, state_ref = refs[5:]
    tile = lax.axis_index("tile")
    core = lax.axis_index("frame")
    beside = neighbour_tile(tile, core, tiles)
    both = state_in_ref[GROUP:, :] + beside_ref[...]
    repeated = dot(both.astype(bf16), repeat_ref[...])
    same_row = iota((8, 1024), 0) == iota((8, 1024), 1) % 8
    for b in range(BINS):
        for g in range(0, COLOURS, 2):
            pair = []
            for i in range(2):
                line = repeated[b * COLOURS + g + i : b * COLOURS + g + i + 1]
                pair.append(jnp.where(same_row, line, 0.0))
            weight_ref[b, 8 * g : 8 * g + 16, :] = jnp.concatenate(pair, axis=0).astype(bf16)
        field_ref[b] = dot(weight_ref[b], pixels_refs[b][...])
    for b in range(BINS):
        rows = slice(b * COLOURS, (b + 1) * COLOURS)
        now = both[rows]
        cross = dot_nt(now, now, exact)
        for g in range(COLOURS):
            column = jnp.broadcast_to(cross[:, g : g + 1], (COLOURS, EDGE))
            cross_ref[(b * COLOURS + g) * 16 : (b * COLOURS + g) * 16 + 16, :] = column
    floor = floor_share * FRAMES

    def update(step, carry):
        b = step // 2
        q = step % 2
        first = b * COLOURS
        row = pl.multiple_of(q * 16, 16)
        states = [
            slab_ref[first + m, pl.ds(row, 16), :].astype(f32) for m in range(COLOURS)
        ]
        for g in range(COLOURS):
            base = (first + g) * 16
            support = states[g] > 0.0
            field = jnp.concatenate(
                [
                    field_ref[b, 8 * g : 8 * g + 8, pl.ds(pl.multiple_of((2 * q + i) * EDGE, EDGE), EDGE)]
                    for i in range(2)
                ],
                axis=0,
            )
            rest = field
            for m in list(range(g, COLOURS)) + list(range(g)):
                rest = rest - cross_ref[pl.ds(base + m, 1), :] * states[m]
            scale = 1.0 / jnp.maximum(cross_ref[pl.ds(base + g, 1), :], floor)
            fresh = jnp.maximum(states[g] + rest * scale, 0.0)
            fresh = jnp.where(support, fresh, 0.0).astype(bf16)
            state_ref[first + g, pl.ds(row, 16), :] = fresh
            states[g] = fresh.astype(f32)
        return carry

    lax.fori_loop(0, 2 * BINS, update, 0)
    for s in range(SLOTS):
        first = (s // LAYERS) * COLOURS
        own_ref[s] = state_ref[first + colour_ref[tile * SLOTS + s]]
        out_ref[s] = state_ref[first + colour_ref[beside * SLOTS + s]]


def patch_kernel(
    rows_ref, cols_ref, colour_ref, state_ref, own_ref, recv_ref, sib_own_ref, sib_recv_ref,
    out_ref, traces_ref, framed_ref, made_ref, sems,
):
    tile = lax.axis_index("tile")
    own = state_ref[GROUP:, :]
    rolled = jnp.concatenate([own[:, 64:], own[:, :64]], axis=1)
    framed_ref[...] = jnp.where(lax.axis_index("frame") == 0, own, rolled)[:, :64]
    core = lax.axis_index("frame")
    line = iota((PATCH, EDGE), 1)
    block = line // HALF
    home = jnp.where(core == 0, HALF, 2 * HALF)
    edge = jnp.where(core == 0, 0, 3 * HALF)
    far_home = 3 * HALF - home
    far_edge = 3 * HALF - edge
    base = jnp.where(block == 0, home, jnp.where(block == 1, edge, jnp.where(block == 2, far_home, far_edge)))
    row_at = base + line % HALF - HALF - iota((PATCH, EDGE), 0)
    col_at = iota((EDGE, PATCH), 0) - iota((EDGE, PATCH), 1)
    writes = []
    for s in range(SLOTS):
        at = (s // LAYERS) * COLOURS + colour_ref[tile * SLOTS + s]
        traces_ref[s : s + 1, :] = framed_ref[pl.ds(at, 1), :]
        row_pick = jnp.where(row_at == rows_ref[s], 1.0, 0.0).astype(bf16)
        col_pick = jnp.where(col_at == cols_ref[s], 1.0, 0.0).astype(bf16)
        whole = jnp.concatenate([own_ref[s], recv_ref[s], sib_own_ref[s], sib_recv_ref[s]], axis=0)
        lifted = dot(row_pick, whole).astype(bf16)
        made_ref[s] = dot(lifted, col_pick).astype(bf16)
        if s % LAYERS == LAYERS - 1:
            part = slice(s - LAYERS + 1, s + 1)
            writes.append(
                pltpu.make_async_copy(made_ref.at[part], out_ref.at[part], sems.at[s // LAYERS])
            )
            writes[-1].start()
    for write in writes:
        write.wait()


def shape(dims, dtype=f32):
    return jax.ShapeDtypeStruct(dims, dtype)


def call(kernel, ins, outs, name, limit, scratch=(), out_specs=None):
    return pl.pallas_call(
        kernel,
        in_specs=ins,
        out_specs=out_specs or [vmem] * len(outs),
        out_shape=outs,
        scratch_shapes=list(scratch),
        name=name,
        compiler_params=pltpu.CompilerParams(vmem_limit_bytes=limit * 2**20),
    )


def on_device(movie_block, patches, patch_rows, patch_cols, neuron_live, neuron_colour, traces):
    tiles = lax.axis_size("tile")
    swap_pairs = []
    for t in range(tiles - 1):
        swap_pairs += [(2 * t + 1, 2 * t + 2), (2 * t + 2, 2 * t + 1)]

    def pair_swap(value):
        return lax.ppermute(value, ("tile", "frame"), swap_pairs)

    far_pairs = [(2 * (tiles - 1) + 1, 2 * (tiles - 3) + 1), (0, 4)]
    for t in range(tiles - 3):
        far_pairs += [(2 * t + 1, 2 * (t + 3)), (2 * (t + 3), 2 * t + 1)]

    def chip_swap(value):
        return lax.ppermute(value, "frame", [(0, 1), (1, 0)])

    def in_hbm(value):
        return pltpu.with_memory_space_constraint(value, pltpu.HBM)

    piece = shape((SLOTS, HALF, EDGE), bf16)
    group = shape((GROUP, FRAMES))
    hbm = pl.BlockSpec(memory_space=pltpu.HBM)
    movie_far = chip_swap(movie_block)
    piece_out, piece_own = call(
        slab_kernel,
        [smem, smem, smem, hbm],
        [piece, piece],
        "slabs",
        8,
        [
            pltpu.VMEM((SLOTS, PATCH, PATCH), bf16),
            pltpu.VMEM((SLOTS, 3 * PATCH, EDGE), f32),
            pltpu.SemaphoreType.DMA((4,)),
        ],
    )(in_hbm(patch_rows), in_hbm(patch_cols), in_hbm(neuron_live), in_hbm(patches))
    piece_recv = pair_swap(piece_out)
    begin, movie_strip = call(
        fetch_kernel,
        [smem, vmem, hbm],
        [shape((SLOTS, 64)), shape((64, HALF, 512), bf16)],
        "fetch",
        4,
        [pltpu.SemaphoreType.DMA((8,))],
    )(in_hbm(neuron_live), in_hbm(traces), in_hbm(movie_block))
    begin_far = chip_swap(begin)

    slab, message, *pixels = call(
        functools.partial(partial_kernel, tiles),
        [smem] + [vmem] * 6,
        [shape((GROUP, HALF, EDGE), bf16), shape((2 * GROUP + COLOURS, FRAMES))]
        + [shape((1024, 512), bf16)] * BINS,
        "partial_sums",
        12,
    )(neuron_colour, movie_strip, movie_far, piece_own, piece_recv, begin, begin_far)

    packed_shape, side_shape = shape((PACKED, FRAMES)), shape((SIDE, FRAMES))
    state_shape = shape((2 * GROUP, FRAMES))
    (packed,) = call(pack_kernel, [vmem] * 2, [packed_shape], "pack", 2)(message, chip_swap(message))
    pair = pair_swap(packed)
    counter = shape((1, 1), jnp.int32)
    phases, repeat, phase_count = call(
        table_kernel,
        [smem, vmem],
        [shape((GROUP, FRAMES), jnp.int32), shape((FRAMES, 1024), bf16), counter],
        "tables",
        2,
        [pltpu.SMEM((GROUP,), jnp.int32)],
    )(neuron_colour, packed)
    (onward,) = call(
        functools.partial(forward_kernel, tiles), [vmem] * 3, [packed_shape], "forward", 2
    )(packed, pair, phases)
    beyond = lax.ppermute(onward, ("tile", "frame"), far_pairs)
    (side,) = call(side_kernel, [vmem] * 3, [side_shape], "side", 2)(packed, pair, beyond)
    state, change, gram, before, beside, left = call(
        window_kernel,
        [vmem] * 5,
        [state_shape, group, shape((2 * COLOURS, FRAMES)), group, group, counter],
        "window",
        8,
    )(phase_count, phases, packed, side, chip_swap(side))

    def advance(carry):
        left, state, before, change, _ = carry
        delta = pair_swap(change)
        state, change, before, left = call(
            next_phase_kernel, [vmem] * 8, [state_shape, group, group, counter], "next_phase", 4
        )(left, phase_count, phases, gram, state, before, delta, chip_swap(delta))
        (beside,) = call(add_kernel, [vmem] * 2, [group], "add", 2)(before, pair_swap(change))
        return left, state, before, change, beside

    carry = (left, state, before, change, beside)
    _, state, _, _, beside = lax.while_loop(lambda c: (c[0] > 0).reshape(()), advance, carry)

    final_out, final_own = call(
        functools.partial(spatial_kernel, tiles),
        [smem] + [vmem] * 8,
        [piece, piece],
        "spatial",
        10,
        [
            pltpu.VMEM((BINS, 128, 1024), bf16),
            pltpu.VMEM((GROUP * COLOURS, EDGE), f32),
            pltpu.VMEM((BINS, 128, 512), f32),
            pltpu.VMEM((GROUP, HALF, EDGE), bf16),
        ],
    )(neuron_colour, repeat, *pixels, slab, state, beside)

    far_own = chip_swap(final_own)
    final_recv = pair_swap(final_out)
    far_recv = chip_swap(final_recv)
    new_patches, new_traces = call(
        patch_kernel,
        [smem] * 3 + [vmem] * 5,
        [shape((SLOTS, PATCH, PATCH), bf16), shape((SLOTS, 64))],
        "patches",
        8,
        [
            pltpu.VMEM((GROUP, 64), f32),
            pltpu.VMEM((SLOTS, PATCH, PATCH), bf16),
            pltpu.SemaphoreType.DMA((BINS,)),
        ],
        [hbm, vmem],
    )(patch_rows, patch_cols, neuron_colour, state, final_own, final_recv, far_own, far_recv)
    return (new_traces, new_patches)


def solution(mesh):
    placed = (
        P("frame", "tile", None),
        P("tile", None, None),
        P("tile"),
        P("tile"),
        P("tile"),
        P(),
        P("tile", "frame"),
    )
    return jax.shard_map(
        on_device,
        mesh=mesh,
        in_specs=placed,
        out_specs=(P("tile", "frame"), P("tile", None, None)),
        check_vma=False,
    )
```

```python
import functools

import jax
import jax.numpy as jnp
from jax import lax
from jax.experimental import pallas as pl
from jax.experimental.pallas import tpu as pltpu
from jax.sharding import PartitionSpec as P

exact = lax.Precision.HIGHEST
f32 = jnp.float32
bf16 = jnp.bfloat16
BINS = 4
LAYERS = 8
SLOTS = 32
COLOURS = 16
PATCH = 64
HALF = 32
EDGE = 128
FRAMES = 128
GROUP = BINS * COLOURS
floor_share = 0.25

vmem = pl.BlockSpec(memory_space=pltpu.VMEM)
smem = pl.BlockSpec(memory_space=pltpu.SMEM)


def iota(shape, dim):
    return lax.broadcasted_iota(jnp.int32, shape, dim)


def dot_nt(a, b, precision=None):
    return lax.dot_general(
        a, b, (((1,), (1,)), ((), ())), precision=precision, preferred_element_type=f32
    )


def dot(a, b, precision=None):
    return lax.dot_general(
        a, b, (((1,), (0,)), ((), ())), precision=precision, preferred_element_type=f32
    )


def neighbour_tile(tile, core, tiles):
    other = jnp.where(core == 0, tile - 1, tile + 1)
    other = jnp.where(other < 0, tile + 1, other)
    return jnp.where(other >= tiles, tile - 1, other)


def slab_kernel(
    rows_ref, cols_ref, live_ref, patches_ref, out_ref, own_ref, raw_ref, pad_ref, sems,
):
    core = lax.axis_index("frame")
    chunk = SLOTS // 4
    fetches = []
    for i in range(4):
        part = slice(i * chunk, (i + 1) * chunk)
        fetches.append(pltpu.make_async_copy(patches_ref.at[part], raw_ref.at[part], sems.at[i]))
        fetches[i].start()
    zeros = jnp.zeros((PATCH, EDGE), f32)
    blank = jnp.zeros((PATCH, PATCH), f32)
    for s in range(SLOTS):
        pad_ref[s, :PATCH, :] = zeros
        pad_ref[s, 2 * PATCH :, :] = zeros
    for s in range(SLOTS):
        if s % chunk == 0:
            fetches[s // chunk].wait()
        filled = jnp.where(live_ref[s] > 0, raw_ref[s].astype(f32), 0.0)
        pad_ref[s, PATCH : 2 * PATCH, :] = jnp.concatenate([filled, blank], axis=1)
        start = jnp.where(core == 0, HALF, PATCH + HALF) - rows_ref[s]
        window = pad_ref[s, pl.ds(start, PATCH), :]
        window = pltpu.roll(window, cols_ref[s], 1).astype(bf16)
        upper, lower = window[:HALF], window[HALF:]
        out_ref[s] = jnp.where(core == 0, upper, lower)
        own_ref[s] = jnp.where(core == 0, lower, upper)


def fetch_kernel(
    live_ref, traces_ref, far_ref, movie_ref, begin_ref, begin_far_ref, strip_ref, sems
):
    first = pl.multiple_of(HALF * lax.axis_index("frame"), HALF)
    fetches = fetch_rows(movie_ref, strip_ref, first, sems)
    for s in range(SLOTS):
        alive = live_ref[s].astype(f32)
        begin_ref[s : s + 1, :] = traces_ref[s : s + 1, :] * alive
        begin_far_ref[s : s + 1, :] = far_ref[s : s + 1, :] * alive
    for fetch in fetches:
        fetch.wait()


def table_kernel(colour_ref, anchor_ref, phase_ref, repeat_ref, count_ref, left_ref, owner_ref):
    tile = lax.axis_index("tile")
    for i in range(GROUP):
        owner_ref[i] = 0
    for s in range(SLOTS):
        at = (s // LAYERS) * COLOURS + colour_ref[tile * SLOTS + s]
        owner_ref[at] = 1
    most = jnp.int32(0)
    for b in range(BINS):
        phase = jnp.int32(0)
        for g in range(COLOURS):
            i = b * COLOURS + g
            if g:
                phase = phase + jnp.abs(owner_ref[i] - owner_ref[i - 1])
            value = phase + 100 * (1 - owner_ref[i])
            phase_ref[i : i + 1, :] = jnp.full((1, FRAMES), value, jnp.int32)
        most = jnp.maximum(most, phase + 1)
    count_ref[...] = jnp.full((1, 1), most, jnp.int32)
    left_ref[...] = jnp.full((1, 1), most - 2, jnp.int32)
    position = (iota((FRAMES, 1024), 1) // 8 + 64 * lax.axis_index("frame")) % FRAMES
    repeat_ref[...] = jnp.where(position == iota((FRAMES, 1024), 0), 1.0, 0.0).astype(bf16)


def fetch_rows(movie_ref, strip_ref, first, sems):
    fetches = []
    for i in range(8):
        part = slice(8 * i, 8 * i + 8)
        rows = movie_ref.at[part, pl.ds(first, HALF), :]
        fetches.append(pltpu.make_async_copy(rows, strip_ref.at[part], sems.at[i]))
        fetches[-1].start()
    return fetches


def strips(ref, items, first, lanes):
    parts = []
    for q in range(HALF // 8):
        part = ref[items, pl.ds(pl.multiple_of(first + 8 * q, 8), 8), lanes]
        parts.append(part.reshape(part.shape[0] * 8, EDGE))
    return jnp.concatenate(parts, axis=1)


def partial_kernel(
    tiles, colour_ref, mine_ref, other_ref, own_ref, recv_ref, near_ref, far_ref,
    slab_ref, message_ref, *pixels_refs,
):
    tile = lax.axis_index("tile")
    core = lax.axis_index("frame")
    beside = neighbour_tile(tile, core, tiles)
    message_ref[...] = jnp.zeros_like(message_ref)
    start = GROUP + COLOURS
    wide = jnp.concatenate([near_ref[...], far_ref[...]], axis=1)
    swapped = jnp.concatenate([far_ref[...], near_ref[...]], axis=1)
    first = jnp.where(core == 0, wide, swapped)
    for s in range(SLOTS):
        b = s // LAYERS
        mine = b * COLOURS + colour_ref[tile * SLOTS + s]
        theirs = b * COLOURS + colour_ref[beside * SLOTS + s]
        slab_ref[mine] = own_ref[s]
        slab_ref[theirs] = recv_ref[s]
        message_ref[pl.ds(start + mine, 1), :] = first[s : s + 1]
    same_row = iota((512, 128), 0) % 8 == iota((512, 128), 1) % 8
    fold = jnp.where(iota((COLOURS, 384), 1) % 128 // 8 == iota((COLOURS, 384), 0), 1.0, 0.0)
    parts = {}
    grams = []
    boths = []
    for i, ref in enumerate((mine_ref, other_ref)):
        for b in range(BINS):
            if i == 0:
                both = strips(slab_ref, slice(b * COLOURS, (b + 1) * COLOURS), 0, slice(0, EDGE))
                boths.append(both)
                square = jnp.where(same_row[:128], dot_nt(both, both), 0.0)
                grams.append(jnp.sum(square.reshape(COLOURS, 8, 128), axis=1))
            pixels = strips(ref, slice(0, 64), i * HALF * core, slice(b * EDGE, (b + 1) * EDGE))
            pixels_refs[b][512 * i : 512 * i + 512, :] = pixels
            product = jnp.where(same_row, dot_nt(pixels, boths[b]), 0.0)
            parts[b, i] = jnp.sum(product.reshape(64, 8, 128), axis=1)
    drives = []
    for b in range(BINS):
        near = jnp.concatenate([parts[b, 0], parts[b, 1]], axis=0)
        far = jnp.concatenate([parts[b, 1], parts[b, 0]], axis=0)
        drives.append(jnp.where(core == 0, near, far))
    drive = dot_nt(fold.astype(bf16), three_parts(jnp.concatenate(drives, axis=0)))
    for b in range(BINS):
        message_ref[b * COLOURS : (b + 1) * COLOURS, :] = drive[:, b * FRAMES : (b + 1) * FRAMES]
    spread = jnp.where(iota((384, EDGE), 0) % 128 // 8 == iota((384, EDGE), 1) % 16, 1.0, 0.0)
    gram = dot(three_parts(jnp.concatenate(grams, axis=0)), spread.astype(bf16))
    lane = iota((COLOURS, EDGE), 1) // COLOURS
    total = jnp.zeros((COLOURS, EDGE), f32)
    for b in range(BINS):
        total = jnp.where(lane == b, gram[b * COLOURS : (b + 1) * COLOURS], total)
    message_ref[GROUP : GROUP + COLOURS, :] = total


def three_parts(value):
    high = value.astype(bf16)
    rest = value - high.astype(f32)
    middle = rest.astype(bf16)
    low = (rest - middle.astype(f32)).astype(bf16)
    return jnp.concatenate([high, middle, low], axis=1)


def block_diagonal(gram):
    tall = jnp.concatenate([gram] * BINS, axis=0)[:, :GROUP]
    keep = iota((GROUP, GROUP), 0) // COLOURS == iota((GROUP, GROUP), 1) // COLOURS
    return jnp.where(keep, tall, 0.0)


def settle(phase_ref, live_ref, gram, residual, current, phase, state_ref, change_ref):
    whole = jnp.concatenate([gram] * BINS, axis=0)
    lane = iota((GROUP, EDGE), 1)
    diag = jnp.sum(jnp.where(lane == iota((GROUP, EDGE), 0), whole, 0.0), axis=1, keepdims=True)
    inverse = 1.0 / (diag + (1.0 - live_ref[...]))
    chosen = phase_ref[...] == phase
    news = []
    changes = []
    for b in range(BINS):
        rows = slice(b * COLOURS, (b + 1) * COLOURS)
        rest, now = residual[rows], current[rows]
        inv, pick = inverse[rows], chosen[rows]
        row_id = iota((COLOURS, FRAMES), 0)
        change = jnp.zeros((COLOURS, FRAMES), f32)
        for g in range(COLOURS):
            at = slice(g, g + 1)
            value = jnp.maximum(now[at] + rest[at] * inv[at], 0.0) - now[at]
            delta = jnp.where(pick[at], value, 0.0)
            lane_at = slice(b * COLOURS + g, b * COLOURS + g + 1)
            column = jnp.broadcast_to(gram[:, lane_at], (COLOURS, FRAMES))
            rest = rest - column * delta
            change = jnp.where(row_id == g, delta, change)
        state_ref[rows, :] = rest
        state_ref[GROUP + b * COLOURS : GROUP + (b + 1) * COLOURS, :] = now + change
        change_ref[rows, :] = change


def pack_kernel(mine_ref, far_ref, out_ref):
    out_ref[:GROUP, :] = mine_ref[:GROUP, :]
    out_ref[GROUP : 2 * GROUP, :] = far_ref[:GROUP, :]
    grams = slice(GROUP, GROUP + COLOURS)
    out_ref[2 * GROUP : 2 * GROUP + COLOURS, :] = mine_ref[grams, :]
    out_ref[2 * GROUP + COLOURS : 2 * GROUP + 2 * COLOURS, :] = far_ref[grams, :]
    out_ref[2 * GROUP + 2 * COLOURS :, :] = mine_ref[GROUP + COLOURS :, :]


near_drive = slice(0, GROUP)
far_drive = slice(GROUP, 2 * GROUP)
near_gram = slice(2 * GROUP, 2 * GROUP + COLOURS)
far_gram = slice(2 * GROUP + COLOURS, 2 * GROUP + 2 * COLOURS)
all_traces = slice(2 * GROUP + 2 * COLOURS, 3 * GROUP + 2 * COLOURS)
PACKED = 3 * GROUP + 2 * COLOURS


def forward_kernel(tiles, pack_ref, pair_ref, anchor_ref, out_ref):
    tile = lax.axis_index("tile")
    core = lax.axis_index("frame")
    last = ((tile == 0) & (core == 0)) | ((tile == tiles - 1) & (core == 1))
    alone = jnp.where(last, 1.0, 0.0)
    out_ref[near_drive, :] = pack_ref[near_drive, :] + pair_ref[near_drive, :]
    out_ref[far_drive, :] = pair_ref[far_drive, :] + alone * pack_ref[far_drive, :]
    out_ref[near_gram, :] = pack_ref[near_gram, :] + pair_ref[near_gram, :]
    out_ref[far_gram, :] = pair_ref[far_gram, :] + alone * pack_ref[far_gram, :]
    out_ref[all_traces, :] = pack_ref[all_traces, :] + pair_ref[all_traces, :]


side_drives = [slice(i * GROUP, (i + 1) * GROUP) for i in range(3)]
side_grams = [slice(3 * GROUP + i * COLOURS, 3 * GROUP + (i + 1) * COLOURS) for i in range(3)]
side_next = slice(3 * GROUP + 3 * COLOURS, 4 * GROUP + 3 * COLOURS)
side_beyond = slice(4 * GROUP + 3 * COLOURS, 5 * GROUP + 3 * COLOURS)
SIDE = 5 * GROUP + 3 * COLOURS


def side_kernel(pack_ref, pair_ref, beyond_ref, out_ref):
    out_ref[side_drives[0], :] = pack_ref[near_drive, :] + pair_ref[near_drive, :]
    out_ref[side_drives[1], :] = pair_ref[far_drive, :] + beyond_ref[far_drive, :]
    out_ref[side_drives[2], :] = beyond_ref[near_drive, :]
    out_ref[side_grams[0], :] = pack_ref[near_gram, :] + pair_ref[near_gram, :]
    out_ref[side_grams[1], :] = pair_ref[far_gram, :] + beyond_ref[far_gram, :]
    out_ref[side_grams[2], :] = beyond_ref[near_gram, :]
    out_ref[side_next, :] = pair_ref[all_traces, :]
    out_ref[side_beyond, :] = beyond_ref[all_traces, :]


def settler(gram):
    whole = jnp.concatenate([gram] * BINS, axis=0)
    diag = jnp.where(iota((GROUP, EDGE), 1) == iota((GROUP, EDGE), 0), whole, 0.0)
    diag = jnp.sum(diag, axis=1, keepdims=True)
    inverse = jnp.broadcast_to(1.0 / jnp.where(diag > 0.0, diag, 1.0), (GROUP, FRAMES))
    row_id = iota((COLOURS, FRAMES), 0)

    def settle(residual, current, chosen):
        rests, changes = [], []
        for b in range(BINS):
            rows = slice(b * COLOURS, (b + 1) * COLOURS)
            rest, now, inv, pick = residual[rows], current[rows], inverse[rows], chosen[rows]
            change = jnp.zeros((COLOURS, FRAMES), f32)
            for g in range(COLOURS):
                at = slice(g, g + 1)
                value = jnp.maximum(now[at] + rest[at] * inv[at], 0.0) - now[at]
                delta = jnp.where(pick[at], value, 0.0)
                lane_at = slice(b * COLOURS + g, b * COLOURS + g + 1)
                rest = rest - jnp.broadcast_to(gram[:, lane_at], (COLOURS, FRAMES)) * delta
                change = jnp.where(row_id == g, delta, change)
            rests.append(rest)
            changes.append(change)
        return jnp.concatenate(rests, axis=0), jnp.concatenate(changes, axis=0)

    return settle


def window_kernel(
    phase_ref, pack_ref, here_ref, there_ref, state_ref, change_ref, gram_ref, before_ref, beside_ref
):
    phase = phase_ref[...]
    own = phase < 100
    start = pack_ref[all_traces, :]
    sides = []
    for ref in (here_ref, there_ref):
        grams = [ref[at, :] for at in side_grams]
        near, beyond = ref[side_next, :], ref[side_beyond, :]
        second = jnp.where(own, beyond, 0.0)
        blocks = [block_diagonal(gram) for gram in grams]
        held = [start + near, near + second, beyond]
        parts = [ref[side_drives[i], :] - dot(blocks[i], held[i], exact) for i in range(3)]
        sides.append((grams, blocks, parts, near, second))
    (grams_a, blocks_a, parts_a, near_a, second_a), (grams_b, blocks_b, parts_b, near_b, second_b) = sides
    mine_now, theirs_now = phase == 0, phase == 100
    settle_own = settler(grams_a[0] + grams_b[0])
    settle_near = settler(grams_a[0] + grams_a[1])
    rest, change = settle_own(parts_a[0] + parts_b[0], start, mine_now)
    rest_a, near_change_a = settle_near(parts_a[0] + parts_a[1], near_a, theirs_now)
    _, near_change_b = settler(grams_b[0] + grams_b[1])(parts_b[0] + parts_b[1], near_b, theirs_now)
    _, second_change = settler(grams_a[1] + grams_a[2])(parts_a[1] + parts_a[2], second_a, mine_now)
    rest = rest - dot(blocks_a[0], near_change_a, exact) - dot(blocks_b[0], near_change_b, exact)
    rest_a = rest_a - dot(blocks_a[0], change, exact) - dot(blocks_a[1], second_change, exact)
    now = start + change
    near_now = near_a + near_change_a
    rest, late = settle_own(rest, now, phase == 1)
    _, near_late = settle_near(rest_a, near_now, phase == 101)
    state_ref[:GROUP, :] = rest
    state_ref[GROUP:, :] = now + late
    change_ref[...] = late
    gram_ref[:COLOURS, :] = grams_a[0]
    gram_ref[COLOURS:, :] = grams_b[0]
    before_ref[...] = near_now
    beside_ref[...] = near_now + near_late


def add_kernel(a_ref, b_ref, out_ref):
    out_ref[...] = a_ref[...] + b_ref[...]


def next_phase_kernel(
    left_ref, count_ref, phase_ref, gram_ref, old_ref, before_ref, delta_ref, far_delta_ref,
    state_ref, change_ref, before_out_ref, left_out_ref,
):
    step = count_ref[...] - left_ref[...]
    left_out_ref[...] = left_ref[...] - 1
    here = gram_ref[:COLOURS, :]
    there = gram_ref[COLOURS:, :]
    coupled = dot(block_diagonal(here), delta_ref[...], exact)
    coupled = coupled + dot(block_diagonal(there), far_delta_ref[...], exact)
    now = old_ref[GROUP:, :]
    chosen = phase_ref[...] == step
    rest, change = settler(here + there)(old_ref[:GROUP, :] - coupled, now, chosen)
    state_ref[:GROUP, :] = rest
    state_ref[GROUP:, :] = now + change
    change_ref[...] = change
    before_out_ref[...] = before_ref[...] + delta_ref[...]


def spatial_kernel(
    tiles, colour_ref, repeat_ref, *refs
):
    pixels_refs, refs = refs[:BINS], refs[BINS:]
    slab_ref, state_in_ref, beside_ref, out_ref, own_ref = refs[:5]
    weight_ref, cross_ref, field_ref, state_ref = refs[5:]
    tile = lax.axis_index("tile")
    core = lax.axis_index("frame")
    beside = neighbour_tile(tile, core, tiles)
    both = state_in_ref[GROUP:, :] + beside_ref[...]
    repeated = dot(both.astype(bf16), repeat_ref[...])
    same_row = iota((8, 1024), 0) == iota((8, 1024), 1) % 8
    for b in range(BINS):
        for g in range(0, COLOURS, 2):
            pair = []
            for i in range(2):
                line = repeated[b * COLOURS + g + i : b * COLOURS + g + i + 1]
                pair.append(jnp.where(same_row, line, 0.0))
            weight_ref[b, 8 * g : 8 * g + 16, :] = jnp.concatenate(pair, axis=0).astype(bf16)
        field_ref[b] = dot(weight_ref[b], pixels_refs[b][...])
    for b in range(BINS):
        rows = slice(b * COLOURS, (b + 1) * COLOURS)
        now = both[rows]
        cross = dot_nt(now, now, exact)
        for g in range(COLOURS):
            column = jnp.broadcast_to(cross[:, g : g + 1], (COLOURS, EDGE))
            cross_ref[(b * COLOURS + g) * 16 : (b * COLOURS + g) * 16 + 16, :] = column
    floor = floor_share * FRAMES

    def update(step, carry):
        b = step // 2
        q = step % 2
        first = b * COLOURS
        row = pl.multiple_of(q * 16, 16)
        states = [
            slab_ref[first + m, pl.ds(row, 16), :].astype(f32) for m in range(COLOURS)
        ]
        for g in range(COLOURS):
            base = (first + g) * 16
            support = states[g] > 0.0
            field = jnp.concatenate(
                [
                    field_ref[b, 8 * g : 8 * g + 8, pl.ds(pl.multiple_of((2 * q + i) * EDGE, EDGE), EDGE)]
                    for i in range(2)
                ],
                axis=0,
            )
            rest = field
            for m in list(range(g, COLOURS)) + list(range(g)):
                rest = rest - cross_ref[pl.ds(base + m, 1), :] * states[m]
            scale = 1.0 / jnp.maximum(cross_ref[pl.ds(base + g, 1), :], floor)
            fresh = jnp.maximum(states[g] + rest * scale, 0.0)
            fresh = jnp.where(support, fresh, 0.0).astype(bf16)
            state_ref[first + g, pl.ds(row, 16), :] = fresh
            states[g] = fresh.astype(f32)
        return carry

    lax.fori_loop(0, 2 * BINS, update, 0)
    for s in range(SLOTS):
        first = (s // LAYERS) * COLOURS
        own_ref[s] = state_ref[first + colour_ref[tile * SLOTS + s]]
        out_ref[s] = state_ref[first + colour_ref[beside * SLOTS + s]]


def patch_kernel(
    rows_ref, cols_ref, own_ref, recv_ref, sib_own_ref, sib_recv_ref, out_ref
):
    core = lax.axis_index("frame")
    line = iota((PATCH, EDGE), 1)
    block = line // HALF
    home = jnp.where(core == 0, HALF, 2 * HALF)
    edge = jnp.where(core == 0, 0, 3 * HALF)
    far_home = 3 * HALF - home
    far_edge = 3 * HALF - edge
    base = jnp.where(block == 0, home, jnp.where(block == 1, edge, jnp.where(block == 2, far_home, far_edge)))
    row_at = base + line % HALF - HALF - iota((PATCH, EDGE), 0)
    col_at = iota((EDGE, PATCH), 0) - iota((EDGE, PATCH), 1)
    for s in range(SLOTS):
        row_pick = jnp.where(row_at == rows_ref[s], 1.0, 0.0).astype(bf16)
        col_pick = jnp.where(col_at == cols_ref[s], 1.0, 0.0).astype(bf16)
        whole = jnp.concatenate([own_ref[s], recv_ref[s], sib_own_ref[s], sib_recv_ref[s]], axis=0)
        lifted = dot(row_pick, whole).astype(bf16)
        out_ref[s] = dot(lifted, col_pick).astype(bf16)


def traces_kernel(colour_ref, state_ref, own_ref, traces_ref, own_out_ref, framed_ref):
    tile = lax.axis_index("tile")
    own = state_ref[GROUP:, :]
    rolled = jnp.concatenate([own[:, 64:], own[:, :64]], axis=1)
    framed_ref[...] = jnp.where(lax.axis_index("frame") == 0, own, rolled)[:, :64]
    for s in range(SLOTS):
        at = (s // LAYERS) * COLOURS + colour_ref[tile * SLOTS + s]
        traces_ref[s : s + 1, :] = framed_ref[pl.ds(at, 1), :]
    own_out_ref[...] = own_ref[...]


def shape(dims, dtype=f32):
    return jax.ShapeDtypeStruct(dims, dtype)


def call(kernel, ins, outs, name, limit, scratch=(), out_specs=None):
    return pl.pallas_call(
        kernel,
        in_specs=ins,
        out_specs=out_specs or [vmem] * len(outs),
        out_shape=outs,
        scratch_shapes=list(scratch),
        name=name,
        compiler_params=pltpu.CompilerParams(vmem_limit_bytes=limit * 2**20),
    )


def on_device(movie_block, patches, patch_rows, patch_cols, neuron_live, neuron_colour, traces):
    tiles = lax.axis_size("tile")
    swap_pairs = []
    for t in range(tiles - 1):
        swap_pairs += [(2 * t + 1, 2 * t + 2), (2 * t + 2, 2 * t + 1)]

    def pair_swap(value):
        return lax.ppermute(value, ("tile", "frame"), swap_pairs)

    far_pairs = [(2 * (tiles - 1) + 1, 2 * (tiles - 3) + 1), (0, 4)]
    for t in range(tiles - 3):
        far_pairs += [(2 * t + 1, 2 * (t + 3)), (2 * (t + 3), 2 * t + 1)]

    def chip_swap(value):
        return lax.ppermute(value, "frame", [(0, 1), (1, 0)])

    def in_hbm(value):
        return pltpu.with_memory_space_constraint(value, pltpu.HBM)

    piece = shape((SLOTS, HALF, EDGE), bf16)
    group = shape((GROUP, FRAMES))
    hbm = pl.BlockSpec(memory_space=pltpu.HBM)
    movie_far = chip_swap(movie_block)
    traces_far = chip_swap(traces)
    piece_out, piece_own = call(
        slab_kernel,
        [smem, smem, smem, hbm],
        [piece, piece],
        "slabs",
        8,
        [
            pltpu.VMEM((SLOTS, PATCH, PATCH), bf16),
            pltpu.VMEM((SLOTS, 3 * PATCH, EDGE), f32),
            pltpu.SemaphoreType.DMA((4,)),
        ],
    )(in_hbm(patch_rows), in_hbm(patch_cols), in_hbm(neuron_live), in_hbm(patches))
    piece_recv = pair_swap(piece_out)
    begin, begin_far, movie_strip = call(
        fetch_kernel,
        [smem, vmem, vmem, hbm],
        [shape((SLOTS, 64)), shape((SLOTS, 64)), shape((64, HALF, 512), bf16)],
        "fetch",
        4,
        [pltpu.SemaphoreType.DMA((8,))],
    )(in_hbm(neuron_live), in_hbm(traces), traces_far, in_hbm(movie_block))

    slab, message, *pixels = call(
        functools.partial(partial_kernel, tiles),
        [smem] + [vmem] * 6,
        [shape((GROUP, HALF, EDGE), bf16), shape((2 * GROUP + COLOURS, FRAMES))]
        + [shape((1024, 512), bf16)] * BINS,
        "partial_sums",
        12,
    )(neuron_colour, movie_strip, movie_far, piece_own, piece_recv, begin, begin_far)

    packed_shape, side_shape = shape((PACKED, FRAMES)), shape((SIDE, FRAMES))
    state_shape = shape((2 * GROUP, FRAMES))
    (packed,) = call(pack_kernel, [vmem] * 2, [packed_shape], "pack", 2)(message, chip_swap(message))
    pair = pair_swap(packed)
    counter = shape((1, 1), jnp.int32)
    phases, repeat, phase_count, left = call(
        table_kernel,
        [smem, vmem],
        [shape((GROUP, FRAMES), jnp.int32), shape((FRAMES, 1024), bf16)]
        + [counter] * 2,
        "tables",
        2,
        [pltpu.SMEM((GROUP,), jnp.int32)],
    )(neuron_colour, packed)
    (onward,) = call(
        functools.partial(forward_kernel, tiles), [vmem] * 3, [packed_shape], "forward", 2
    )(packed, pair, phases)
    beyond = lax.ppermute(onward, ("tile", "frame"), far_pairs)
    (side,) = call(side_kernel, [vmem] * 3, [side_shape], "side", 2)(packed, pair, beyond)
    state, change, gram, before, beside = call(
        window_kernel,
        [vmem] * 4,
        [state_shape, group, shape((2 * COLOURS, FRAMES)), group, group],
        "window",
        8,
    )(phases, packed, side, chip_swap(side))

    def advance(carry):
        left, state, before, change, _ = carry
        delta = pair_swap(change)
        state, change, before, left = call(
            next_phase_kernel, [vmem] * 8, [state_shape, group, group, counter], "next_phase", 4
        )(left, phase_count, phases, gram, state, before, delta, chip_swap(delta))
        (beside,) = call(add_kernel, [vmem] * 2, [group], "add", 2)(before, pair_swap(change))
        return left, state, before, change, beside

    carry = (left, state, before, change, beside)
    _, state, _, _, beside = lax.while_loop(lambda c: (c[0] > 0).reshape(()), advance, carry)

    final_out, final_own = call(
        functools.partial(spatial_kernel, tiles),
        [smem] + [vmem] * 8,
        [piece, piece],
        "spatial",
        10,
        [
            pltpu.VMEM((BINS, 128, 1024), bf16),
            pltpu.VMEM((GROUP * COLOURS, EDGE), f32),
            pltpu.VMEM((BINS, 128, 512), f32),
            pltpu.VMEM((GROUP, HALF, EDGE), bf16),
        ],
    )(neuron_colour, repeat, *pixels, slab, state, beside)

    new_traces, kept_own = call(
        traces_kernel,
        [smem, vmem, vmem],
        [shape((SLOTS, 64)), piece],
        "traces",
        2,
        [pltpu.VMEM((GROUP, 64), f32)],
    )(neuron_colour, state, final_own)
    far_own = chip_swap(kept_own)
    final_recv = pair_swap(final_out)
    far_recv = chip_swap(final_recv)
    (new_patches,) = call(
        patch_kernel, [smem, smem] + [vmem] * 4, [shape((SLOTS, PATCH, PATCH), bf16)], "patches", 8
    )(patch_rows, patch_cols, kept_own, final_recv, far_own, far_recv)
    return (new_traces, new_patches)


def solution(mesh):
    placed = (
        P("frame", "tile", None),
        P("tile", None, None),
        P("tile"),
        P("tile"),
        P("tile"),
        P(),
        P("tile", "frame"),
    )
    return jax.shard_map(
        on_device,
        mesh=mesh,
        in_specs=placed,
        out_specs=(P("tile", "frame"), P("tile", None, None)),
        check_vma=False,
    )
```

```python
import functools

import jax
import jax.numpy as jnp
from jax import lax
from jax.experimental import pallas as pl
from jax.experimental.pallas import tpu as pltpu
from jax.sharding import PartitionSpec as P

exact = lax.Precision.HIGHEST
f32 = jnp.float32
bf16 = jnp.bfloat16
BINS = 4
LAYERS = 8
SLOTS = 32
COLOURS = 16
PATCH = 64
HALF = 32
EDGE = 128
FRAMES = 128
GROUP = BINS * COLOURS
floor_share = 0.25

vmem = pl.BlockSpec(memory_space=pltpu.VMEM)
smem = pl.BlockSpec(memory_space=pltpu.SMEM)


def iota(shape, dim):
    return lax.broadcasted_iota(jnp.int32, shape, dim)


def dot_nt(a, b, precision=None):
    return lax.dot_general(
        a, b, (((1,), (1,)), ((), ())), precision=precision, preferred_element_type=f32
    )


def dot(a, b, precision=None):
    return lax.dot_general(
        a, b, (((1,), (0,)), ((), ())), precision=precision, preferred_element_type=f32
    )


def neighbour_tile(tile, core, tiles):
    other = jnp.where(core == 0, tile - 1, tile + 1)
    other = jnp.where(other < 0, tile + 1, other)
    return jnp.where(other >= tiles, tile - 1, other)


def slab_kernel(
    rows_ref, cols_ref, live_ref, patches_ref, out_ref, own_ref, raw_ref, pad_ref, sems,
):
    core = lax.axis_index("frame")
    chunk = SLOTS // 4
    fetches = []
    for i in range(4):
        part = slice(i * chunk, (i + 1) * chunk)
        fetches.append(pltpu.make_async_copy(patches_ref.at[part], raw_ref.at[part], sems.at[i]))
        fetches[i].start()
    zeros = jnp.zeros((PATCH, EDGE), f32)
    blank = jnp.zeros((PATCH, PATCH), f32)
    for s in range(SLOTS):
        pad_ref[s, :PATCH, :] = zeros
        pad_ref[s, 2 * PATCH :, :] = zeros
    for s in range(SLOTS):
        if s % chunk == 0:
            fetches[s // chunk].wait()
        filled = jnp.where(live_ref[s] > 0, raw_ref[s].astype(f32), 0.0)
        pad_ref[s, PATCH : 2 * PATCH, :] = jnp.concatenate([filled, blank], axis=1)
        start = jnp.where(core == 0, HALF, PATCH + HALF) - rows_ref[s]
        window = pad_ref[s, pl.ds(start, PATCH), :]
        window = pltpu.roll(window, cols_ref[s], 1).astype(bf16)
        upper, lower = window[:HALF], window[HALF:]
        out_ref[s] = jnp.where(core == 0, upper, lower)
        own_ref[s] = jnp.where(core == 0, lower, upper)


def fetch_kernel(
    live_ref, traces_ref, far_ref, movie_ref, begin_ref, begin_far_ref, strip_ref, sems
):
    first = pl.multiple_of(HALF * lax.axis_index("frame"), HALF)
    fetches = fetch_rows(movie_ref, strip_ref, first, sems)
    for s in range(SLOTS):
        alive = live_ref[s].astype(f32)
        begin_ref[s : s + 1, :] = traces_ref[s : s + 1, :] * alive
        begin_far_ref[s : s + 1, :] = far_ref[s : s + 1, :] * alive
    for fetch in fetches:
        fetch.wait()


def table_kernel(colour_ref, anchor_ref, phase_ref, repeat_ref, count_ref, left_ref, owner_ref):
    tile = lax.axis_index("tile")
    for i in range(GROUP):
        owner_ref[i] = 0
    for s in range(SLOTS):
        at = (s // LAYERS) * COLOURS + colour_ref[tile * SLOTS + s]
        owner_ref[at] = 1
    most = jnp.int32(0)
    for b in range(BINS):
        phase = jnp.int32(0)
        for g in range(COLOURS):
            i = b * COLOURS + g
            if g:
                phase = phase + jnp.abs(owner_ref[i] - owner_ref[i - 1])
            value = phase + 100 * (1 - owner_ref[i])
            phase_ref[i : i + 1, :] = jnp.full((1, FRAMES), value, jnp.int32)
        most = jnp.maximum(most, phase + 1)
    count_ref[...] = jnp.full((1, 1), most, jnp.int32)
    left_ref[...] = jnp.full((1, 1), most - 2, jnp.int32)
    position = (iota((FRAMES, 1024), 1) // 8 + 64 * lax.axis_index("frame")) % FRAMES
    repeat_ref[...] = jnp.where(position == iota((FRAMES, 1024), 0), 1.0, 0.0).astype(bf16)


def fetch_rows(movie_ref, strip_ref, first, sems):
    fetches = []
    for i in range(8):
        part = slice(8 * i, 8 * i + 8)
        rows = movie_ref.at[part, pl.ds(first, HALF), :]
        fetches.append(pltpu.make_async_copy(rows, strip_ref.at[part], sems.at[i]))
        fetches[-1].start()
    return fetches


def strips(ref, items, first, lanes):
    parts = []
    for q in range(HALF // 8):
        part = ref[items, pl.ds(pl.multiple_of(first + 8 * q, 8), 8), lanes]
        parts.append(part.reshape(part.shape[0] * 8, EDGE))
    return jnp.concatenate(parts, axis=1)


def partial_kernel(
    tiles, colour_ref, mine_ref, other_ref, own_ref, recv_ref, near_ref, far_ref,
    slab_ref, message_ref, *pixels_refs,
):
    tile = lax.axis_index("tile")
    core = lax.axis_index("frame")
    beside = neighbour_tile(tile, core, tiles)
    message_ref[...] = jnp.zeros_like(message_ref)
    start = GROUP + COLOURS
    wide = jnp.concatenate([near_ref[...], far_ref[...]], axis=1)
    swapped = jnp.concatenate([far_ref[...], near_ref[...]], axis=1)
    first = jnp.where(core == 0, wide, swapped)
    for s in range(SLOTS):
        b = s // LAYERS
        mine = b * COLOURS + colour_ref[tile * SLOTS + s]
        theirs = b * COLOURS + colour_ref[beside * SLOTS + s]
        slab_ref[mine] = own_ref[s]
        slab_ref[theirs] = recv_ref[s]
        message_ref[pl.ds(start + mine, 1), :] = first[s : s + 1]
    same_row = iota((512, 128), 0) % 8 == iota((512, 128), 1) % 8
    fold = jnp.where(iota((COLOURS, 384), 1) % 128 // 8 == iota((COLOURS, 384), 0), 1.0, 0.0)
    parts = {}
    grams = []
    boths = []
    for i, ref in enumerate((mine_ref, other_ref)):
        for b in range(BINS):
            if i == 0:
                both = strips(slab_ref, slice(b * COLOURS, (b + 1) * COLOURS), 0, slice(0, EDGE))
                boths.append(both)
                square = jnp.where(same_row[:128], dot_nt(both, both), 0.0)
                grams.append(jnp.sum(square.reshape(COLOURS, 8, 128), axis=1))
            pixels = strips(ref, slice(0, 64), i * HALF * core, slice(b * EDGE, (b + 1) * EDGE))
            pixels_refs[b][512 * i : 512 * i + 512, :] = pixels
            product = jnp.where(same_row, dot_nt(pixels, boths[b]), 0.0)
            parts[b, i] = jnp.sum(product.reshape(64, 8, 128), axis=1)
    drives = []
    for b in range(BINS):
        near = jnp.concatenate([parts[b, 0], parts[b, 1]], axis=0)
        far = jnp.concatenate([parts[b, 1], parts[b, 0]], axis=0)
        drives.append(jnp.where(core == 0, near, far))
    drive = dot_nt(fold.astype(bf16), three_parts(jnp.concatenate(drives, axis=0)))
    for b in range(BINS):
        message_ref[b * COLOURS : (b + 1) * COLOURS, :] = drive[:, b * FRAMES : (b + 1) * FRAMES]
    spread = jnp.where(iota((384, EDGE), 0) % 128 // 8 == iota((384, EDGE), 1) % 16, 1.0, 0.0)
    gram = dot(three_parts(jnp.concatenate(grams, axis=0)), spread.astype(bf16))
    lane = iota((COLOURS, EDGE), 1) // COLOURS
    total = jnp.zeros((COLOURS, EDGE), f32)
    for b in range(BINS):
        total = jnp.where(lane == b, gram[b * COLOURS : (b + 1) * COLOURS], total)
    message_ref[GROUP : GROUP + COLOURS, :] = total


def three_parts(value):
    high = value.astype(bf16)
    rest = value - high.astype(f32)
    middle = rest.astype(bf16)
    low = (rest - middle.astype(f32)).astype(bf16)
    return jnp.concatenate([high, middle, low], axis=1)


def block_diagonal(gram):
    tall = jnp.concatenate([gram] * BINS, axis=0)[:, :GROUP]
    keep = iota((GROUP, GROUP), 0) // COLOURS == iota((GROUP, GROUP), 1) // COLOURS
    return jnp.where(keep, tall, 0.0)


def settle(phase_ref, live_ref, gram, residual, current, phase, state_ref, change_ref):
    whole = jnp.concatenate([gram] * BINS, axis=0)
    lane = iota((GROUP, EDGE), 1)
    diag = jnp.sum(jnp.where(lane == iota((GROUP, EDGE), 0), whole, 0.0), axis=1, keepdims=True)
    inverse = 1.0 / (diag + (1.0 - live_ref[...]))
    chosen = phase_ref[...] == phase
    news = []
    changes = []
    for b in range(BINS):
        rows = slice(b * COLOURS, (b + 1) * COLOURS)
        rest, now = residual[rows], current[rows]
        inv, pick = inverse[rows], chosen[rows]
        row_id = iota((COLOURS, FRAMES), 0)
        change = jnp.zeros((COLOURS, FRAMES), f32)
        for g in range(COLOURS):
            at = slice(g, g + 1)
            value = jnp.maximum(now[at] + rest[at] * inv[at], 0.0) - now[at]
            delta = jnp.where(pick[at], value, 0.0)
            lane_at = slice(b * COLOURS + g, b * COLOURS + g + 1)
            column = jnp.broadcast_to(gram[:, lane_at], (COLOURS, FRAMES))
            rest = rest - column * delta
            change = jnp.where(row_id == g, delta, change)
        state_ref[rows, :] = rest
        state_ref[GROUP + b * COLOURS : GROUP + (b + 1) * COLOURS, :] = now + change
        change_ref[rows, :] = change


def pack_kernel(mine_ref, far_ref, out_ref):
    out_ref[:GROUP, :] = mine_ref[:GROUP, :]
    out_ref[GROUP : 2 * GROUP, :] = far_ref[:GROUP, :]
    grams = slice(GROUP, GROUP + COLOURS)
    out_ref[2 * GROUP : 2 * GROUP + COLOURS, :] = mine_ref[grams, :]
    out_ref[2 * GROUP + COLOURS : 2 * GROUP + 2 * COLOURS, :] = far_ref[grams, :]
    out_ref[2 * GROUP + 2 * COLOURS :, :] = mine_ref[GROUP + COLOURS :, :]


near_drive = slice(0, GROUP)
far_drive = slice(GROUP, 2 * GROUP)
near_gram = slice(2 * GROUP, 2 * GROUP + COLOURS)
far_gram = slice(2 * GROUP + COLOURS, 2 * GROUP + 2 * COLOURS)
all_traces = slice(2 * GROUP + 2 * COLOURS, 3 * GROUP + 2 * COLOURS)
PACKED = 3 * GROUP + 2 * COLOURS


def forward_kernel(tiles, pack_ref, pair_ref, anchor_ref, out_ref):
    tile = lax.axis_index("tile")
    core = lax.axis_index("frame")
    last = ((tile == 0) & (core == 0)) | ((tile == tiles - 1) & (core == 1))
    alone = jnp.where(last, 1.0, 0.0)
    out_ref[near_drive, :] = pack_ref[near_drive, :] + pair_ref[near_drive, :]
    out_ref[far_drive, :] = pair_ref[far_drive, :] + alone * pack_ref[far_drive, :]
    out_ref[near_gram, :] = pack_ref[near_gram, :] + pair_ref[near_gram, :]
    out_ref[far_gram, :] = pair_ref[far_gram, :] + alone * pack_ref[far_gram, :]
    out_ref[all_traces, :] = pack_ref[all_traces, :] + pair_ref[all_traces, :]


side_drives = [slice(i * GROUP, (i + 1) * GROUP) for i in range(3)]
side_grams = [slice(3 * GROUP + i * COLOURS, 3 * GROUP + (i + 1) * COLOURS) for i in range(3)]
side_next = slice(3 * GROUP + 3 * COLOURS, 4 * GROUP + 3 * COLOURS)
side_beyond = slice(4 * GROUP + 3 * COLOURS, 5 * GROUP + 3 * COLOURS)
SIDE = 5 * GROUP + 3 * COLOURS


def side_kernel(pack_ref, pair_ref, beyond_ref, out_ref):
    out_ref[side_drives[0], :] = pack_ref[near_drive, :] + pair_ref[near_drive, :]
    out_ref[side_drives[1], :] = pair_ref[far_drive, :] + beyond_ref[far_drive, :]
    out_ref[side_drives[2], :] = beyond_ref[near_drive, :]
    out_ref[side_grams[0], :] = pack_ref[near_gram, :] + pair_ref[near_gram, :]
    out_ref[side_grams[1], :] = pair_ref[far_gram, :] + beyond_ref[far_gram, :]
    out_ref[side_grams[2], :] = beyond_ref[near_gram, :]
    out_ref[side_next, :] = pair_ref[all_traces, :]
    out_ref[side_beyond, :] = beyond_ref[all_traces, :]


def settler(gram):
    whole = jnp.concatenate([gram] * BINS, axis=0)
    diag = jnp.where(iota((GROUP, EDGE), 1) == iota((GROUP, EDGE), 0), whole, 0.0)
    diag = jnp.sum(diag, axis=1, keepdims=True)
    inverse = jnp.broadcast_to(1.0 / jnp.where(diag > 0.0, diag, 1.0), (GROUP, FRAMES))
    row_id = iota((COLOURS, FRAMES), 0)

    def settle(residual, current, chosen):
        rests, changes = [], []
        for b in range(BINS):
            rows = slice(b * COLOURS, (b + 1) * COLOURS)
            rest, now, inv, pick = residual[rows], current[rows], inverse[rows], chosen[rows]
            change = jnp.zeros((COLOURS, FRAMES), f32)
            for g in range(COLOURS):
                at = slice(g, g + 1)
                value = jnp.maximum(now[at] + rest[at] * inv[at], 0.0) - now[at]
                delta = jnp.where(pick[at], value, 0.0)
                lane_at = slice(b * COLOURS + g, b * COLOURS + g + 1)
                rest = rest - jnp.broadcast_to(gram[:, lane_at], (COLOURS, FRAMES)) * delta
                change = jnp.where(row_id == g, delta, change)
            rests.append(rest)
            changes.append(change)
        return jnp.concatenate(rests, axis=0), jnp.concatenate(changes, axis=0)

    return settle


def window_kernel(
    phase_ref, pack_ref, here_ref, there_ref, state_ref, change_ref, gram_ref, before_ref, beside_ref
):
    phase = phase_ref[...]
    own = phase < 100
    start = pack_ref[all_traces, :]
    sides = []
    for ref in (here_ref, there_ref):
        grams = [ref[at, :] for at in side_grams]
        near, beyond = ref[side_next, :], ref[side_beyond, :]
        second = jnp.where(own, beyond, 0.0)
        blocks = [block_diagonal(gram) for gram in grams]
        held = [start + near, near + second, beyond]
        parts = [ref[side_drives[i], :] - dot(blocks[i], held[i], exact) for i in range(3)]
        sides.append((grams, blocks, parts, near, second))
    (grams_a, blocks_a, parts_a, near_a, second_a), (grams_b, blocks_b, parts_b, near_b, second_b) = sides
    mine_now, theirs_now = phase == 0, phase == 100
    settle_own = settler(grams_a[0] + grams_b[0])
    settle_near = settler(grams_a[0] + grams_a[1])
    rest, change = settle_own(parts_a[0] + parts_b[0], start, mine_now)
    rest_a, near_change_a = settle_near(parts_a[0] + parts_a[1], near_a, theirs_now)
    _, near_change_b = settler(grams_b[0] + grams_b[1])(parts_b[0] + parts_b[1], near_b, theirs_now)
    _, second_change = settler(grams_a[1] + grams_a[2])(parts_a[1] + parts_a[2], second_a, mine_now)
    rest = rest - dot(blocks_a[0], near_change_a, exact) - dot(blocks_b[0], near_change_b, exact)
    rest_a = rest_a - dot(blocks_a[0], change, exact) - dot(blocks_a[1], second_change, exact)
    now = start + change
    near_now = near_a + near_change_a
    rest, late = settle_own(rest, now, phase == 1)
    _, near_late = settle_near(rest_a, near_now, phase == 101)
    state_ref[:GROUP, :] = rest
    state_ref[GROUP:, :] = now + late
    change_ref[...] = late
    gram_ref[:COLOURS, :] = grams_a[0]
    gram_ref[COLOURS:, :] = grams_b[0]
    before_ref[...] = near_now
    beside_ref[...] = near_now + near_late


def add_kernel(a_ref, b_ref, out_ref):
    out_ref[...] = a_ref[...] + b_ref[...]


def next_phase_kernel(
    left_ref, count_ref, phase_ref, gram_ref, old_ref, before_ref, delta_ref, far_delta_ref,
    state_ref, change_ref, before_out_ref, left_out_ref,
):
    step = count_ref[...] - left_ref[...]
    left_out_ref[...] = left_ref[...] - 1
    here = gram_ref[:COLOURS, :]
    there = gram_ref[COLOURS:, :]
    coupled = dot(block_diagonal(here), delta_ref[...], exact)
    coupled = coupled + dot(block_diagonal(there), far_delta_ref[...], exact)
    now = old_ref[GROUP:, :]
    chosen = phase_ref[...] == step
    rest, change = settler(here + there)(old_ref[:GROUP, :] - coupled, now, chosen)
    state_ref[:GROUP, :] = rest
    state_ref[GROUP:, :] = now + change
    change_ref[...] = change
    before_out_ref[...] = before_ref[...] + delta_ref[...]


def spatial_kernel(
    tiles, colour_ref, repeat_ref, *refs
):
    pixels_refs, refs = refs[:BINS], refs[BINS:]
    slab_ref, state_in_ref, beside_ref, out_ref, own_ref = refs[:5]
    weight_ref, cross_ref, field_ref, state_ref = refs[5:]
    tile = lax.axis_index("tile")
    core = lax.axis_index("frame")
    beside = neighbour_tile(tile, core, tiles)
    both = state_in_ref[GROUP:, :] + beside_ref[...]
    repeated = dot(both.astype(bf16), repeat_ref[...])
    same_row = iota((8, 1024), 0) == iota((8, 1024), 1) % 8
    for b in range(BINS):
        for g in range(0, COLOURS, 2):
            pair = []
            for i in range(2):
                line = repeated[b * COLOURS + g + i : b * COLOURS + g + i + 1]
                pair.append(jnp.where(same_row, line, 0.0))
            weight_ref[b, 8 * g : 8 * g + 16, :] = jnp.concatenate(pair, axis=0).astype(bf16)
        field_ref[b] = dot(weight_ref[b], pixels_refs[b][...])
    for b in range(BINS):
        rows = slice(b * COLOURS, (b + 1) * COLOURS)
        now = both[rows]
        cross = dot_nt(now, now, exact)
        for g in range(COLOURS):
            column = jnp.broadcast_to(cross[:, g : g + 1], (COLOURS, EDGE))
            cross_ref[(b * COLOURS + g) * 16 : (b * COLOURS + g) * 16 + 16, :] = column
    floor = floor_share * FRAMES

    def update(step, carry):
        b = step // 2
        q = step % 2
        first = b * COLOURS
        row = pl.multiple_of(q * 16, 16)
        states = [
            slab_ref[first + m, pl.ds(row, 16), :].astype(f32) for m in range(COLOURS)
        ]
        for g in range(COLOURS):
            base = (first + g) * 16
            support = states[g] > 0.0
            field = jnp.concatenate(
                [
                    field_ref[b, 8 * g : 8 * g + 8, pl.ds(pl.multiple_of((2 * q + i) * EDGE, EDGE), EDGE)]
                    for i in range(2)
                ],
                axis=0,
            )
            rest = field
            for m in list(range(g, COLOURS)) + list(range(g)):
                rest = rest - cross_ref[pl.ds(base + m, 1), :] * states[m]
            scale = 1.0 / jnp.maximum(cross_ref[pl.ds(base + g, 1), :], floor)
            fresh = jnp.maximum(states[g] + rest * scale, 0.0)
            fresh = jnp.where(support, fresh, 0.0).astype(bf16)
            state_ref[first + g, pl.ds(row, 16), :] = fresh
            states[g] = fresh.astype(f32)
        return carry

    lax.fori_loop(0, 2 * BINS, update, 0, unroll=2)
    for s in range(SLOTS):
        first = (s // LAYERS) * COLOURS
        own_ref[s] = state_ref[first + colour_ref[tile * SLOTS + s]]
        out_ref[s] = state_ref[first + colour_ref[beside * SLOTS + s]]


def patch_kernel(
    rows_ref, cols_ref, own_ref, recv_ref, sib_own_ref, sib_recv_ref, out_ref
):
    core = lax.axis_index("frame")
    line = iota((PATCH, EDGE), 1)
    block = line // HALF
    home = jnp.where(core == 0, HALF, 2 * HALF)
    edge = jnp.where(core == 0, 0, 3 * HALF)
    far_home = 3 * HALF - home
    far_edge = 3 * HALF - edge
    base = jnp.where(block == 0, home, jnp.where(block == 1, edge, jnp.where(block == 2, far_home, far_edge)))
    row_at = base + line % HALF - HALF - iota((PATCH, EDGE), 0)
    col_at = iota((EDGE, PATCH), 0) - iota((EDGE, PATCH), 1)
    for s in range(SLOTS):
        row_pick = jnp.where(row_at == rows_ref[s], 1.0, 0.0).astype(bf16)
        col_pick = jnp.where(col_at == cols_ref[s], 1.0, 0.0).astype(bf16)
        whole = jnp.concatenate([own_ref[s], recv_ref[s], sib_own_ref[s], sib_recv_ref[s]], axis=0)
        lifted = dot(row_pick, whole).astype(bf16)
        out_ref[s] = dot(lifted, col_pick).astype(bf16)


def traces_kernel(colour_ref, state_ref, own_ref, traces_ref, own_out_ref, framed_ref):
    tile = lax.axis_index("tile")
    own = state_ref[GROUP:, :]
    rolled = jnp.concatenate([own[:, 64:], own[:, :64]], axis=1)
    framed_ref[...] = jnp.where(lax.axis_index("frame") == 0, own, rolled)[:, :64]
    for s in range(SLOTS):
        at = (s // LAYERS) * COLOURS + colour_ref[tile * SLOTS + s]
        traces_ref[s : s + 1, :] = framed_ref[pl.ds(at, 1), :]
    own_out_ref[...] = own_ref[...]


def shape(dims, dtype=f32):
    return jax.ShapeDtypeStruct(dims, dtype)


def call(kernel, ins, outs, name, limit, scratch=(), out_specs=None):
    return pl.pallas_call(
        kernel,
        in_specs=ins,
        out_specs=out_specs or [vmem] * len(outs),
        out_shape=outs,
        scratch_shapes=list(scratch),
        name=name,
        compiler_params=pltpu.CompilerParams(vmem_limit_bytes=limit * 2**20),
    )


def on_device(movie_block, patches, patch_rows, patch_cols, neuron_live, neuron_colour, traces):
    tiles = lax.axis_size("tile")
    swap_pairs = []
    for t in range(tiles - 1):
        swap_pairs += [(2 * t + 1, 2 * t + 2), (2 * t + 2, 2 * t + 1)]

    def pair_swap(value):
        return lax.ppermute(value, ("tile", "frame"), swap_pairs)

    far_pairs = [(2 * (tiles - 1) + 1, 2 * (tiles - 3) + 1), (0, 4)]
    for t in range(tiles - 3):
        far_pairs += [(2 * t + 1, 2 * (t + 3)), (2 * (t + 3), 2 * t + 1)]

    def chip_swap(value):
        return lax.ppermute(value, "frame", [(0, 1), (1, 0)])

    def in_hbm(value):
        return pltpu.with_memory_space_constraint(value, pltpu.HBM)

    piece = shape((SLOTS, HALF, EDGE), bf16)
    group = shape((GROUP, FRAMES))
    hbm = pl.BlockSpec(memory_space=pltpu.HBM)
    movie_far = chip_swap(movie_block)
    traces_far = chip_swap(traces)
    piece_out, piece_own = call(
        slab_kernel,
        [smem, smem, smem, hbm],
        [piece, piece],
        "slabs",
        8,
        [
            pltpu.VMEM((SLOTS, PATCH, PATCH), bf16),
            pltpu.VMEM((SLOTS, 3 * PATCH, EDGE), f32),
            pltpu.SemaphoreType.DMA((4,)),
        ],
    )(in_hbm(patch_rows), in_hbm(patch_cols), in_hbm(neuron_live), in_hbm(patches))
    piece_recv = pair_swap(piece_out)
    begin, begin_far, movie_strip = call(
        fetch_kernel,
        [smem, vmem, vmem, hbm],
        [shape((SLOTS, 64)), shape((SLOTS, 64)), shape((64, HALF, 512), bf16)],
        "fetch",
        4,
        [pltpu.SemaphoreType.DMA((8,))],
    )(in_hbm(neuron_live), in_hbm(traces), traces_far, in_hbm(movie_block))

    slab, message, *pixels = call(
        functools.partial(partial_kernel, tiles),
        [smem] + [vmem] * 6,
        [shape((GROUP, HALF, EDGE), bf16), shape((2 * GROUP + COLOURS, FRAMES))]
        + [shape((1024, 512), bf16)] * BINS,
        "partial_sums",
        12,
    )(neuron_colour, movie_strip, movie_far, piece_own, piece_recv, begin, begin_far)

    packed_shape, side_shape = shape((PACKED, FRAMES)), shape((SIDE, FRAMES))
    state_shape = shape((2 * GROUP, FRAMES))
    (packed,) = call(pack_kernel, [vmem] * 2, [packed_shape], "pack", 2)(message, chip_swap(message))
    pair = pair_swap(packed)
    counter = shape((1, 1), jnp.int32)
    phases, repeat, phase_count, left = call(
        table_kernel,
        [smem, vmem],
        [shape((GROUP, FRAMES), jnp.int32), shape((FRAMES, 1024), bf16)]
        + [counter] * 2,
        "tables",
        2,
        [pltpu.SMEM((GROUP,), jnp.int32)],
    )(neuron_colour, packed)
    (onward,) = call(
        functools.partial(forward_kernel, tiles), [vmem] * 3, [packed_shape], "forward", 2
    )(packed, pair, phases)
    beyond = lax.ppermute(onward, ("tile", "frame"), far_pairs)
    (side,) = call(side_kernel, [vmem] * 3, [side_shape], "side", 2)(packed, pair, beyond)
    state, change, gram, before, beside = call(
        window_kernel,
        [vmem] * 4,
        [state_shape, group, shape((2 * COLOURS, FRAMES)), group, group],
        "window",
        8,
    )(phases, packed, side, chip_swap(side))

    def advance(carry):
        left, state, before, change, _ = carry
        delta = pair_swap(change)
        state, change, before, left = call(
            next_phase_kernel, [vmem] * 8, [state_shape, group, group, counter], "next_phase", 4
        )(left, phase_count, phases, gram, state, before, delta, chip_swap(delta))
        (beside,) = call(add_kernel, [vmem] * 2, [group], "add", 2)(before, pair_swap(change))
        return left, state, before, change, beside

    carry = (left, state, before, change, beside)
    _, state, _, _, beside = lax.while_loop(lambda c: (c[0] > 0).reshape(()), advance, carry)

    final_out, final_own = call(
        functools.partial(spatial_kernel, tiles),
        [smem] + [vmem] * 8,
        [piece, piece],
        "spatial",
        10,
        [
            pltpu.VMEM((BINS, 128, 1024), bf16),
            pltpu.VMEM((GROUP * COLOURS, EDGE), f32),
            pltpu.VMEM((BINS, 128, 512), f32),
            pltpu.VMEM((GROUP, HALF, EDGE), bf16),
        ],
    )(neuron_colour, repeat, *pixels, slab, state, beside)

    new_traces, kept_own = call(
        traces_kernel,
        [smem, vmem, vmem],
        [shape((SLOTS, 64)), piece],
        "traces",
        2,
        [pltpu.VMEM((GROUP, 64), f32)],
    )(neuron_colour, state, final_own)
    far_own = chip_swap(kept_own)
    final_recv = pair_swap(final_out)
    far_recv = chip_swap(final_recv)
    (new_patches,) = call(
        patch_kernel, [smem, smem] + [vmem] * 4, [shape((SLOTS, PATCH, PATCH), bf16)], "patches", 8
    )(patch_rows, patch_cols, kept_own, final_recv, far_own, far_recv)
    return (new_traces, new_patches)


def solution(mesh):
    placed = (
        P("frame", "tile", None),
        P("tile", None, None),
        P("tile"),
        P("tile"),
        P("tile"),
        P(),
        P("tile", "frame"),
    )
    return jax.shard_map(
        on_device,
        mesh=mesh,
        in_specs=placed,
        out_specs=(P("tile", "frame"), P("tile", None, None)),
        check_vma=False,
    )
```
